32 devices in a mesh: groups: 2 (over y), param: 4 (over z), example: 2 (over x), sub: 2 (over core).
Axes of the slice: x: 2, y: 2, z: 4, core: 2. Of those that a mesh axis runs over, the one named last changes fastest.
Arguments:
- grads: bfloat16 [128, 32768], P(('groups', 'example'), ('param', 'sub')), parts along dimension 0, may hold values from -6 to 6
- seeds: int32 [65536], P(('groups', 'param', 'sub')), parts along dimension 0, may hold values from 0 to 4194303
- adam_table: float32 [4, 16384], P(None, ('groups', 'param', 'sub')), parts along dimension 1, may hold values from 0.1 to 1
- ckpt_index: int32 [128], P(('groups', 'example')), parts along dimension 0, may hold values from 0 to 3
Outputs:
- influence: float32 [128, 64], P(('groups', 'example'), ('param', 'sub')), parts along dimension 0
The draws below stay inside these ranges and needn't reach their ends.
There are 2 independent parts, one for each index of `groups`. The reference program is written for one: setup_inputs(seed, part) draws one part's arguments, and reference() takes and returns one part's arrays. A program takes and returns all parts, laid end to end along the dimension named above; each array names one. Nothing has to cross between parts.
All inputs are finite; a program needn't handle non-finite values.
Results may differ from the reference program's by a relative error of at most 0.0039.
Values may be sent and summed in bfloat16 or wider, within the bound.
A program may use at most 64 MiB of HBM per device.

```python
import math
import jax
import jax.numpy as jnp
from jax import lax

K = 8192
CKPT = 4
P_SIZE = 32768
E = 64


def touch_ends(entries, rng, low, largest):
    longest = entries.shape.index(max(entries.shape))
    spots = []
    for shift in (0, 1):
        where = [jax.random.randint(jax.random.fold_in(rng, axis), (), 0, length) for axis, length in enumerate(entries.shape)]
        where[longest] = (where[longest] + shift) % entries.shape[longest]
        spots.append(tuple(where))
    return entries.at[spots[0]].set(low).at[spots[1]].set(largest)


def strengthened(entries, key, source, target, parts, factor):
    owner, partner = [(jnp.arange(entries.shape[dim]) // (entries.shape[dim] // parts)).reshape([-1 if axis == dim else 1 for axis in range(entries.ndim)]) for dim in (source, target)]
    chosen = jax.random.permutation(key, parts)[partner]
    strong = (owner == chosen) | (owner == (partner + parts // 2) % parts)
    return jnp.where(strong, factor * entries, entries)


def block_scale(own_key, extent, cuts, low, high):
    def one(axis_at, blocks):
        heights = jax.random.uniform(jax.random.fold_in(jax.random.fold_in(own_key, 6), axis_at), (blocks,), jnp.float32, low / len(cuts), high / len(cuts))
        return jnp.repeat(jnp.exp(heights), extent[axis_at] // blocks).reshape((-1,) + (1,) * (len(extent) - axis_at - 1))

    gain = one(*cuts[0])
    for cut in cuts[1:]:
        gain = gain * one(*cut)
    return gain


def heavy_noise(key, shape, width, limit, shards, heavy, kind=jnp.bfloat16):
    drawn = width * jax.random.normal(key, shape, jnp.float32)
    if shards:
        drawn = drawn * block_scale(key, shape, shards, -0.22, 0.18)
    return jnp.clip(strengthened(drawn, jax.random.fold_in(key, 3), *heavy), -limit, limit).astype(kind)


def setup_inputs(seed: int = 0, part: int = 0) -> dict:
    arg_keys = jax.random.split(jax.random.key(seed), 5)
    own_keys = jax.random.split(jax.random.fold_in(arg_keys[4], part), 5)
    grads = heavy_noise(own_keys[0], (E, P_SIZE), 1.0, 6.0, ((0, 2), (1, 8)), (1, 0, 8, 2.0))
    seeds = touch_ends(jax.random.randint(own_keys[1], (P_SIZE,), 0, 4194304), jax.random.fold_in(own_keys[1], 1), 0, 4194303).astype(jnp.int32)
    adam_table = jnp.clip(jnp.exp(math.log(1.0) - 2.3025851 * jax.random.uniform(own_keys[2], (CKPT, K), jnp.float32) ** block_scale(own_keys[2], (CKPT, K), ((1, 8),), -0.2, 0.2)), 0.1, 1.0)
    ckpt_index = touch_ends(jax.random.randint(own_keys[3], (E,), 0, CKPT), jax.random.fold_in(own_keys[3], 1), 0, CKPT - 1).astype(jnp.int32)
    return dict(grads=grads, seeds=seeds, adam_table=adam_table, ckpt_index=ckpt_index)


def signs_of(seed_block, feature_ids):
    mixed = seed_block[:, None] + feature_ids[None, :] * jnp.int32(1640531527)
    mixed = mixed ^ lax.shift_right_logical(mixed, jnp.int32(16))
    mixed = mixed * jnp.int32(2146121005)
    mixed = mixed ^ lax.shift_right_logical(mixed, jnp.int32(15))
    mixed = mixed * jnp.int32(625341585)
    mixed = mixed ^ lax.shift_right_logical(mixed, jnp.int32(16))
    return (1 - 2 * (mixed & 1)).astype(jnp.bfloat16)

def reference(grads, seeds, adam_table, ckpt_index):
    block_len = min(P_SIZE, 1024)
    block_count = P_SIZE // block_len
    feature_ids = jnp.arange(K, dtype=jnp.int32)

    def accumulate(running, block_no):
        begin = (block_no * block_len).astype(jnp.int32)
        seed_block = lax.dynamic_slice_in_dim(seeds, begin, block_len, 0)
        grad_block = lax.dynamic_slice_in_dim(grads, begin, block_len, 1)
        sign_block = signs_of(seed_block, feature_ids)
        term = lax.dot_general(sign_block, grad_block, (((0,), (1,)), ((), ())), preferred_element_type=jnp.float32)
        return (running + term, None)
    start_sum = jnp.zeros((K, E), jnp.float32)
    summed, _ = lax.scan(accumulate, start_sum, jnp.arange(block_count, dtype=jnp.int32))
    projected = summed * (1.0 / math.sqrt(P_SIZE))
    plain = projected.astype(jnp.bfloat16)
    onehot = (ckpt_index[:, None] == jnp.arange(CKPT, dtype=jnp.int32)[None, :]).astype(jnp.float32)
    scale = jnp.dot(onehot, adam_table, precision=lax.Precision.HIGHEST)
    scaled = (projected * scale.T).astype(jnp.bfloat16)
    pairs = lax.dot_general(scaled, plain, (((0,), (0,)), ((), ())), preferred_element_type=jnp.float32)
    influence = pairs * (1.0 / math.sqrt(K))
    row_ids = jnp.arange(E, dtype=jnp.int32)
    return jnp.where(row_ids[:, None] == row_ids[None, :], jnp.zeros_like(influence), influence)
```

```python
import functools
import math

import jax
import jax.numpy as jnp
from jax import lax
from jax.experimental import pallas as pl
from jax.experimental.pallas import tpu as pltpu
from jax.sharding import PartitionSpec as P

K = 8192
CKPT = 4
STEP = 1640531527
FIRST = 2146121005
SECOND = ((625341585 + 65536) << 15) & 0xFFFFFFFF
SECOND = SECOND - (1 << 32) if SECOND >= 1 << 31 else SECOND
TILE = 256
ROWS = 2048
PIECES = 4
HASHED = 1024
KEPT = (5, 3)
MESH = pl.DeviceIdType.MESH


def sign_tile(seed_tile, offsets):
    mixed = seed_tile + offsets
    mixed = mixed ^ lax.shift_right_logical(mixed, jnp.int32(16))
    mixed = mixed * jnp.int32(FIRST)
    mixed = mixed ^ lax.shift_right_logical(mixed, jnp.int32(15))
    mixed = mixed * jnp.int32(SECOND)
    return jnp.where(mixed < 0, jnp.bfloat16(-1.0), jnp.bfloat16(1.0))


def hash_kernel(seeds_ref, offsets_ref, grads_ref, out_ref, wide_ref):
    e_all, p_local = grads_ref.shape
    wide_ref[...] = jnp.broadcast_to(seeds_ref[...], wide_ref.shape)

    @pl.loop(0, out_ref.shape[1] // TILE)
    def _(block):
        columns = pl.ds(pl.multiple_of(block * TILE, TILE), TILE)
        offsets = offsets_ref[:, columns]

        def add(part, total):
            rows = pl.ds(pl.multiple_of(part * TILE, TILE), TILE)
            seed_tile = wide_ref[rows, :]
            halves = [sign_tile(seed_tile, offsets[:, i : i + 128]) for i in range(0, TILE, 128)]
            return total + jnp.dot(
                grads_ref[:, rows], jnp.concatenate(halves, axis=1), preferred_element_type=jnp.float32
            )

        out_ref[:, columns] = lax.fori_loop(
            0, p_local // TILE, add, jnp.zeros((e_all, TILE), jnp.float32)
        )


def features_of(example, n_c, n_e):
    width = K // (n_c * n_e)
    owner = jnp.arange(n_c, dtype=jnp.int32)[:, None] * (width * n_e)
    return (owner + example * width + jnp.arange(width, dtype=jnp.int32)[None, :]).reshape(1, -1)


def separate(grads, seeds, adam_table, ckpt_index):
    e_local, p_local = grads.shape
    n_c, n_e = lax.axis_size(("param", "sub")), lax.axis_size("example")
    p_whole = p_local * n_c
    width = K // (n_c * n_e)
    example = lax.axis_index("example")
    everyone = lax.all_gather(grads, "example", axis=0, tiled=True)
    index = lax.all_gather(ckpt_index, "example", axis=0, tiled=True)
    e_all = e_local * n_e
    partial = pl.pallas_call(
        hash_kernel,
        out_shape=jax.ShapeDtypeStruct((e_all, n_c * width), jnp.float32),
        in_specs=[pl.BlockSpec(memory_space=pltpu.VMEM)] * 3,
        out_specs=pl.BlockSpec(memory_space=pltpu.VMEM),
        scratch_shapes=[pltpu.VMEM((p_local, 128), jnp.int32)],
        compiler_params=pltpu.CompilerParams(vmem_limit_bytes=40 << 20),
    )(seeds[:, None], features_of(example, n_c, n_e) * jnp.int32(STEP), everyone)
    summed = lax.psum_scatter(partial, ("param", "sub"), scatter_dimension=1, tiled=True)
    projected = summed * (1.0 / math.sqrt(p_whole))
    table = lax.dynamic_slice_in_dim(adam_table, example * width, width, 1)
    onehot = (index[:, None] == jnp.arange(CKPT, dtype=jnp.int32)[None, :]).astype(jnp.float32)
    scale = jnp.dot(onehot, table, precision=lax.Precision.HIGHEST)
    plain = projected.astype(jnp.bfloat16)
    scaled = (projected * scale).astype(jnp.bfloat16)
    pairs = lax.dot_general(scaled, plain, (((1,), (1,)), ((), ())), preferred_element_type=jnp.float32)
    pairs = lax.psum_scatter(pairs, "example", scatter_dimension=0, tiled=True)
    pairs = lax.psum_scatter(pairs, ("param", "sub"), scatter_dimension=1, tiled=True)
    influence = pairs * (1.0 / math.sqrt(K))
    cols = pairs.shape[1]
    row_ids = example * e_local + jnp.arange(e_local, dtype=jnp.int32)
    col_ids = lax.axis_index(("param", "sub")) * cols + jnp.arange(cols, dtype=jnp.int32)
    return jnp.where(row_ids[:, None] == col_ids[None, :], jnp.zeros_like(influence), influence)


def flipped(index, mask, size):
    bits = [1 << i for i in range((size - 1).bit_length())]
    return sum((((index // b) % 2 + (mask // b) % 2) % 2) * b for b in bits) if bits else index


def fused_kernel(
    sizes, seeds_hbm, table_hbm, index_hbm, grads_hbm, out_ref,
    seeds_ref, table_ref, signs_ref, load_sems, wide_ref, all_ref, who_ref, part_ref, near_ref, far_ref, pair_ref, block_ref,
    grad_send, grad_recv, who_send, who_recv, near_send, near_recv, far_send, far_recv, pair_send, pair_recv,
):
    n_p, n_e, n_s, p_whole = sizes
    n_c = n_p * n_s
    e_local, p_local = grads_hbm.shape
    e_all = n_e * e_local
    width = part_ref.shape[2]
    cols = out_ref.shape[0]
    piece = p_local // PIECES
    param, example, sub = lax.axis_index("param"), lax.axis_index("example"), lax.axis_index("sub")
    me = param * n_s + sub

    def device(c_mask, e_mask):
        return {
            "param": flipped(param, c_mask // n_s, n_p),
            "example": flipped(example, e_mask, n_e),
            "sub": flipped(sub, c_mask % n_s, n_s),
        }

    barrier = pltpu.get_barrier_semaphore()
    for mask in range(1, n_c * n_e):
        pl.semaphore_signal(barrier, inc=1, device_id=device(mask % n_c, mask // n_c), device_id_type=MESH)
    mine = pl.ds(pl.multiple_of(example * e_local, e_local), e_local)
    loads = [
        pltpu.make_async_copy(source, target, load_sems.at[i])
        for i, (source, target) in enumerate((
            (seeds_hbm, seeds_ref),
            (grads_hbm, all_ref.at[mine]),
            (index_hbm, who_ref.at[example]),
            (table_hbm, table_ref),
        ))
    ]
    for load in loads:
        load.start()

    def offsets_of(c_mask, block):
        first = (flipped(me, c_mask, n_c) * n_e + example) * width + block * TILE
        return (first + lax.broadcasted_iota(jnp.int32, (1, TILE), 1)) * jnp.int32(STEP)

    def signs_of(seed_tile, offsets):
        return jnp.concatenate(
            [sign_tile(seed_tile, offsets[:, i : i + 128]) for i in range(0, TILE, 128)], axis=1
        )

    loads[0].wait()
    turned = seeds_ref[...].T

    def first_signs(begin, end):
        offsets = offsets_of(KEPT[0], 0)
        for row in range(begin, end):
            rows = slice(row * 128, (row + 1) * 128)
            seed_tile = jnp.broadcast_to(turned[:, row : row + 1], (128, 128))
            wide_ref[rows, :] = seed_tile
            signs_ref[0, rows, :] = signs_of(seed_tile, offsets)

    groups = p_local // 128
    first_signs(0, groups // 4)
    pl.semaphore_wait(barrier, n_c * n_e - 1)
    grad_copies, who_copies = [], []
    for mask in range(1, n_e):
        copy = pltpu.make_async_remote_copy(
            src_ref=index_hbm, dst_ref=who_ref.at[example], send_sem=who_send.at[mask - 1],
            recv_sem=who_recv.at[mask - 1], device_id=device(0, mask), device_id_type=MESH,
        )
        who_copies.append(copy)
        for i in range(PIECES):
            span = pl.ds(i * piece, piece)
            copy = pltpu.make_async_remote_copy(
                src_ref=grads_hbm.at[:, span], dst_ref=all_ref.at[mine, span],
                send_sem=grad_send.at[mask - 1, i], recv_sem=grad_recv.at[mask - 1, i],
                device_id=device(0, mask), device_id_type=MESH,
            )
            copy.start()
            grad_copies.append((i, copy))
    for copy in who_copies:
        copy.start()
    first_signs(groups // 4, groups)
    for kept in KEPT:
        part_ref[kept] = jnp.zeros((e_all, width), jnp.float32)

    @pl.loop(1, 4)
    def _(slot):
        offsets = offsets_of(jnp.where(slot < 2, KEPT[0], KEPT[1]), slot % 2)

        @pl.loop(0, p_local // HASHED)
        def _(part):
            rows = pl.ds(pl.multiple_of(part * HASHED, HASHED), HASHED)
            signs_ref[slot, rows, :] = signs_of(wide_ref[rows, :], offsets)

    for load in loads[1:]:
        load.wait()

    def near_copy(z_mask):
        return pltpu.make_async_remote_copy(
            src_ref=part_ref.at[z_mask * 2 + 1], dst_ref=near_ref.at[z_mask], send_sem=near_send.at[z_mask],
            recv_sem=near_recv.at[z_mask], device_id=device(1, 0), device_id_type=MESH,
        )

    def far_copy(z_mask):
        return pltpu.make_async_remote_copy(
            src_ref=part_ref.at[z_mask * 2], dst_ref=far_ref.at[z_mask - 1], send_sem=far_send.at[z_mask - 1],
            recv_sem=far_recv.at[z_mask - 1], device_id=device(z_mask * 2, 0), device_id_type=MESH,
        )

    def join(z_mask):
        near_copy(z_mask).wait_recv()
        part_ref[z_mask * 2] += near_ref[z_mask]
        far_copy(z_mask).start()

    def chunk(c_mask, block, before, extra):
        offsets = offsets_of(c_mask, block)

        def add(part, running):
            before(part)
            rows = pl.ds(pl.multiple_of(part * ROWS, ROWS), ROWS)
            term = running + jnp.dot(
                all_ref[:, rows], signs_of(wide_ref[rows, :], offsets), preferred_element_type=jnp.float32
            )
            extra(part)
            return term

        span = pl.ds(pl.multiple_of(block * TILE, TILE), TILE)
        part_ref[c_mask, :, span] = lax.fori_loop(
            0, p_local // ROWS, add, jnp.zeros((e_all, TILE), jnp.float32)
        )

    for number, copy in grad_copies:
        if number < PIECES // 2:
            copy.wait_recv()

    @pl.loop(0, 4)
    def _(step):
        c_mask = jnp.where(step == 0, 7, 8 - 2 * step)
        kept = jnp.where(step < 2, KEPT[0], KEPT[1])
        kept_span = pl.ds(pl.multiple_of((step % 2) * TILE, TILE), TILE)

        @pl.loop(0, 2)
        def _(block):
            def before(part):
                @pl.when((step == 0) & (block == 0) & (part == 1))
                def _():
                    for number, copy in grad_copies:
                        if number >= PIECES // 2:
                            copy.wait_recv()

            def extra(part):
                rows = pl.ds(
                    pl.multiple_of(block * (p_local // 2) + part * (ROWS // 2), ROWS // 2), ROWS // 2
                )
                part_ref[kept, :, kept_span] += jnp.dot(
                    all_ref[:, rows], signs_ref[step, rows, :], preferred_element_type=jnp.float32
                )

            chunk(c_mask, block, before, extra)

        @pl.when(step == 0)
        def _():
            near_copy(3).start()

        @pl.when(step == 1)
        def _():
            near_copy(2).start()
            join(3)

        @pl.when(step == 2)
        def _():
            join(2)

        @pl.when(step == 3)
        def _():
            near_copy(1).start()

    @pl.loop(0, 4)
    def _(step):
        chunk(1 - step // 2, step % 2, lambda part: None, lambda part: None)

        @pl.when(step == 0)
        def _():
            join(1)

        @pl.when(step == 1)
        def _():
            near_copy(0).start()

    for copy in who_copies:
        copy.wait_recv()
    summed = part_ref[0]
    for z_mask in range(n_p - 1, 0, -1):
        far_copy(z_mask).wait_recv()
        summed = summed + far_ref[z_mask - 1]
    near_copy(0).wait_recv()
    summed = summed + near_ref[0]
    projected = summed * (1.0 / math.sqrt(p_whole))
    own = pl.ds(pl.multiple_of(example * width, 128), width)
    who = jnp.concatenate(
        [jnp.broadcast_to(who_ref[i], (8, e_local)).T[:, 0:1] for i in range(n_e)], axis=0
    )
    scale = jnp.zeros_like(projected)
    for row in range(CKPT):
        scale = jnp.where(who == row, table_ref[row : row + 1, own], scale)
    plain = projected.astype(jnp.bfloat16)
    scaled = (projected * scale).astype(jnp.bfloat16)
    lanes = pair_ref.shape[1]
    if lanes > e_all:
        scaled = jnp.concatenate([scaled, jnp.zeros((lanes - e_all, width), jnp.bfloat16)], axis=0)
    pair_ref[...] = lax.dot_general(
        plain, scaled, (((1,), (1,)), ((), ())), preferred_element_type=jnp.float32
    )

    copies = []
    for mask in range(n_c * n_e - 1, 0, -1):
        c_mask, e_mask = mask % n_c, mask // n_c
        rows = pl.ds(pl.multiple_of(flipped(me, c_mask, n_c) * cols, cols), cols)
        copy = pltpu.make_async_remote_copy(
            src_ref=pair_ref.at[rows], dst_ref=block_ref.at[mask - 1], send_sem=pair_send.at[mask - 1],
            recv_sem=pair_recv.at[mask - 1], device_id=device(c_mask, e_mask), device_id_type=MESH,
        )
        copy.start()
        copies.append((mask, copy))
    pairs = pair_ref[pl.ds(pl.multiple_of(me * cols, cols), cols), :]
    for mask, copy in copies[::-1]:
        copy.wait_recv()
        pairs = pairs + block_ref[mask - 1]
    block = pairs[:, :e_local]
    for i in range(1, n_e):
        block = jnp.where(example == i, pairs[:, i * e_local : (i + 1) * e_local], block)
    block = block * (1.0 / math.sqrt(K))
    col_ids = me * cols + lax.broadcasted_iota(jnp.int32, block.shape, 0)
    row_ids = example * e_local + lax.broadcasted_iota(jnp.int32, block.shape, 1)
    out_ref[...] = jnp.where(row_ids == col_ids, jnp.zeros_like(block), block)
    for mask, copy in copies:
        copy.wait_send()
    for z_mask in range(n_p):
        near_copy(z_mask).wait_send()
    for z_mask in range(1, n_p):
        far_copy(z_mask).wait_send()
    for number, copy in grad_copies:
        copy.wait_send()
    for copy in who_copies:
        copy.wait_send()


def fused(grads, seeds, adam_table, ckpt_index):
    e_local, p_local = grads.shape
    n_p, n_e, n_s = (lax.axis_size(name) for name in ("param", "example", "sub"))
    n_c = n_p * n_s
    e_all = e_local * n_e
    width = K // (n_c * n_e)
    cols = e_all // n_c
    lanes = -(-e_all // 128) * 128
    dma = pltpu.SemaphoreType.DMA
    return pl.pallas_call(
        functools.partial(fused_kernel, (n_p, n_e, n_s, p_local * n_c)),
        out_shape=jax.ShapeDtypeStruct((cols, e_local), jnp.float32),
        in_specs=[pl.BlockSpec(memory_space=pltpu.HBM)] * 4,
        out_specs=pl.BlockSpec(memory_space=pltpu.VMEM),
        scratch_shapes=[
            pltpu.VMEM((p_local // 128, 128), jnp.int32),
            pltpu.VMEM(adam_table.shape, jnp.float32),
            pltpu.VMEM((4, p_local, TILE), jnp.bfloat16),
            dma((4,)),
            pltpu.VMEM((p_local, 128), jnp.int32),
            pltpu.VMEM((e_all, p_local), jnp.bfloat16),
            pltpu.VMEM((n_e, 1, e_local), jnp.int32),
            pltpu.VMEM((n_c, e_all, width), jnp.float32),
            pltpu.VMEM((n_p, e_all, width), jnp.float32),
            pltpu.VMEM((n_p - 1, e_all, width), jnp.float32),
            pltpu.VMEM((e_all, lanes), jnp.float32),
            pltpu.VMEM((n_c * n_e - 1, cols, lanes), jnp.float32),
            dma((n_e - 1, PIECES)),
            dma((n_e - 1, PIECES)),
            dma((n_e - 1,)),
            dma((n_e - 1,)),
            dma((n_p,)),
            dma((n_p,)),
            dma((n_p - 1,)),
            dma((n_p - 1,)),
            dma((n_c * n_e - 1,)),
            dma((n_c * n_e - 1,)),
        ],
        compiler_params=pltpu.CompilerParams(
            collective_id=0, has_side_effects=True, vmem_limit_bytes=67043328
        ),
    )(
        seeds.reshape(p_local // 128, 128),
        adam_table,
        ckpt_index.reshape(1, e_local),
        grads,
    ).T


def per_device(grads, seeds, adam_table, ckpt_index):
    e_local, p_local = grads.shape
    n_c, n_e = lax.axis_size(("param", "sub")), lax.axis_size("example")
    width, cols = K // (n_c * n_e), e_local * n_e // n_c
    n_p, n_s = lax.axis_size("param"), lax.axis_size("sub")
    if (n_p, n_e, n_s) == (4, 2, 2) and width == 2 * TILE and p_local == 2 * ROWS and cols % 8 == 0:
        return fused(grads, seeds, adam_table, ckpt_index)
    return separate(grads, seeds, adam_table, ckpt_index)


def solution(mesh):
    placed = (
        P(("groups", "example"), ("param", "sub")),
        P(("groups", "param", "sub")),
        P(None, ("groups", "param", "sub")),
        P(("groups", "example")),
    )
    return jax.shard_map(
        per_device,
        mesh=mesh,
        in_specs=placed,
        out_specs=P(("groups", "example"), ("param", "sub")),
        check_vma=False,
    )
```

```python
import functools
import math

import jax
import jax.numpy as jnp
from jax import lax
from jax.experimental import pallas as pl
from jax.experimental.pallas import tpu as pltpu
from jax.sharding import PartitionSpec as P

K = 8192
CKPT = 4
STEP = 1640531527
FIRST = 2146121005
SECOND = ((625341585 + 65536) << 15) & 0xFFFFFFFF
SECOND = SECOND - (1 << 32) if SECOND >= 1 << 31 else SECOND
TILE = 256
ROWS = 2048
PIECES = 4
KEPT = 6
SEGMENT = 1024
MESH = pl.DeviceIdType.MESH


def sign_tile(seed_tile, offsets):
    mixed = seed_tile + offsets
    mixed = mixed ^ lax.shift_right_logical(mixed, jnp.int32(16))
    mixed = mixed * jnp.int32(FIRST)
    mixed = mixed ^ lax.shift_right_logical(mixed, jnp.int32(15))
    mixed = mixed * jnp.int32(SECOND)
    return jnp.where(mixed < 0, jnp.bfloat16(-1.0), jnp.bfloat16(1.0))


def hash_kernel(seeds_ref, offsets_ref, grads_ref, out_ref, wide_ref):
    e_all, p_local = grads_ref.shape
    wide_ref[...] = jnp.broadcast_to(seeds_ref[...], wide_ref.shape)

    @pl.loop(0, out_ref.shape[1] // TILE)
    def _(block):
        columns = pl.ds(pl.multiple_of(block * TILE, TILE), TILE)
        offsets = offsets_ref[:, columns]

        def add(part, total):
            rows = pl.ds(pl.multiple_of(part * TILE, TILE), TILE)
            seed_tile = wide_ref[rows, :]
            halves = [sign_tile(seed_tile, offsets[:, i : i + 128]) for i in range(0, TILE, 128)]
            return total + jnp.dot(
                grads_ref[:, rows], jnp.concatenate(halves, axis=1), preferred_element_type=jnp.float32
            )

        out_ref[:, columns] = lax.fori_loop(
            0, p_local // TILE, add, jnp.zeros((e_all, TILE), jnp.float32)
        )


def features_of(example, n_c, n_e):
    width = K // (n_c * n_e)
    owner = jnp.arange(n_c, dtype=jnp.int32)[:, None] * (width * n_e)
    return (owner + example * width + jnp.arange(width, dtype=jnp.int32)[None, :]).reshape(1, -1)


def separate(grads, seeds, adam_table, ckpt_index):
    e_local, p_local = grads.shape
    n_c, n_e = lax.axis_size(("param", "sub")), lax.axis_size("example")
    p_whole = p_local * n_c
    width = K // (n_c * n_e)
    example = lax.axis_index("example")
    everyone = lax.all_gather(grads, "example", axis=0, tiled=True)
    index = lax.all_gather(ckpt_index, "example", axis=0, tiled=True)
    e_all = e_local * n_e
    partial = pl.pallas_call(
        hash_kernel,
        out_shape=jax.ShapeDtypeStruct((e_all, n_c * width), jnp.float32),
        in_specs=[pl.BlockSpec(memory_space=pltpu.VMEM)] * 3,
        out_specs=pl.BlockSpec(memory_space=pltpu.VMEM),
        scratch_shapes=[pltpu.VMEM((p_local, 128), jnp.int32)],
        compiler_params=pltpu.CompilerParams(vmem_limit_bytes=40 << 20),
    )(seeds[:, None], features_of(example, n_c, n_e) * jnp.int32(STEP), everyone)
    summed = lax.psum_scatter(partial, ("param", "sub"), scatter_dimension=1, tiled=True)
    projected = summed * (1.0 / math.sqrt(p_whole))
    table = lax.dynamic_slice_in_dim(adam_table, example * width, width, 1)
    onehot = (index[:, None] == jnp.arange(CKPT, dtype=jnp.int32)[None, :]).astype(jnp.float32)
    scale = jnp.dot(onehot, table, precision=lax.Precision.HIGHEST)
    plain = projected.astype(jnp.bfloat16)
    scaled = (projected * scale).astype(jnp.bfloat16)
    pairs = lax.dot_general(scaled, plain, (((1,), (1,)), ((), ())), preferred_element_type=jnp.float32)
    pairs = lax.psum_scatter(pairs, "example", scatter_dimension=0, tiled=True)
    pairs = lax.psum_scatter(pairs, ("param", "sub"), scatter_dimension=1, tiled=True)
    influence = pairs * (1.0 / math.sqrt(K))
    cols = pairs.shape[1]
    row_ids = example * e_local + jnp.arange(e_local, dtype=jnp.int32)
    col_ids = lax.axis_index(("param", "sub")) * cols + jnp.arange(cols, dtype=jnp.int32)
    return jnp.where(row_ids[:, None] == col_ids[None, :], jnp.zeros_like(influence), influence)


def flipped(index, mask, size):
    bits = [1 << i for i in range((size - 1).bit_length())]
    return sum((((index // b) % 2 + (mask // b) % 2) % 2) * b for b in bits) if bits else index


def fused_kernel(
    sizes, seeds_hbm, table_hbm, index_hbm, grads_hbm, out_ref,
    seeds_ref, table_ref, signs_ref, load_sems, wide_ref, all_ref, who_ref, part_ref, fresh_ref, held_ref, near_ref, far_ref, pair_ref, block_ref,
    grad_send, grad_recv, who_send, who_recv, near_send, near_recv, far_send, far_recv, pair_send, pair_recv,
):
    n_p, n_e, n_s, p_whole = sizes
    n_c = n_p * n_s
    e_local, p_local = grads_hbm.shape
    e_all = n_e * e_local
    width = part_ref.shape[2]
    cols = out_ref.shape[0]
    piece = p_local // PIECES
    param, example, sub = lax.axis_index("param"), lax.axis_index("example"), lax.axis_index("sub")
    me = param * n_s + sub

    def device(c_mask, e_mask):
        return {
            "param": flipped(param, c_mask // n_s, n_p),
            "example": flipped(example, e_mask, n_e),
            "sub": flipped(sub, c_mask % n_s, n_s),
        }

    barrier = pltpu.get_barrier_semaphore()
    for mask in range(1, n_c * n_e):
        pl.semaphore_signal(barrier, inc=1, device_id=device(mask % n_c, mask // n_c), device_id_type=MESH)
    mine = pl.ds(pl.multiple_of(example * e_local, e_local), e_local)
    loads = [
        pltpu.make_async_copy(source, target, load_sems.at[i])
        for i, (source, target) in enumerate((
            (seeds_hbm, seeds_ref),
            (grads_hbm, all_ref.at[mine]),
            (index_hbm, who_ref.at[example]),
            (table_hbm, table_ref),
        ))
    ]
    for load in loads:
        load.start()

    def offsets_of(c_mask, block):
        first = (flipped(me, c_mask, n_c) * n_e + example) * width + block * TILE
        return (first + lax.broadcasted_iota(jnp.int32, (1, TILE), 1)) * jnp.int32(STEP)

    def signs_of(seed_tile, offsets):
        return jnp.concatenate(
            [sign_tile(seed_tile, offsets[:, i : i + 128]) for i in range(0, TILE, 128)], axis=1
        )

    last = n_c - 1
    loads[0].wait()
    turned = seeds_ref[...].T
    offsets = offsets_of(last, 1)
    for row in range(p_local // 128):
        rows = slice(row * 128, (row + 1) * 128)
        seed_tile = jnp.broadcast_to(turned[:, row : row + 1], (128, 128))
        wide_ref[rows, :] = seed_tile
        signs_ref[0, rows, :] = signs_of(seed_tile, offsets)
    pl.semaphore_wait(barrier, n_c * n_e - 1)
    grad_copies, who_copies = [], []
    for mask in range(1, n_e):
        copy = pltpu.make_async_remote_copy(
            src_ref=index_hbm, dst_ref=who_ref.at[example], send_sem=who_send.at[mask - 1],
            recv_sem=who_recv.at[mask - 1], device_id=device(0, mask), device_id_type=MESH,
        )
        who_copies.append(copy)
        for i in range(PIECES):
            span = pl.ds(i * piece, piece)
            copy = pltpu.make_async_remote_copy(
                src_ref=grads_hbm.at[:, span], dst_ref=all_ref.at[mine, span],
                send_sem=grad_send.at[mask - 1, i], recv_sem=grad_recv.at[mask - 1, i],
                device_id=device(0, mask), device_id_type=MESH,
            )
            copy.start()
            grad_copies.append((i, copy))
    for copy in who_copies:
        copy.start()

    @pl.loop(1, KEPT)
    def _(slot):
        offsets = offsets_of(last - slot, lax.rem(slot + 1, 2))
        signs_ref[slot] = signs_of(wide_ref[...], offsets)

    for load in loads[1:]:
        load.wait()

    def near_copy(z_mask):
        return pltpu.make_async_remote_copy(
            src_ref=part_ref.at[z_mask * 2 + 1], dst_ref=near_ref.at[z_mask], send_sem=near_send.at[z_mask],
            recv_sem=near_recv.at[z_mask], device_id=device(1, 0), device_id_type=MESH,
        )

    def far_copy(z_mask):
        return pltpu.make_async_remote_copy(
            src_ref=part_ref.at[z_mask * 2], dst_ref=far_ref.at[z_mask - 1], send_sem=far_send.at[z_mask - 1],
            recv_sem=far_recv.at[z_mask - 1], device_id=device(z_mask * 2, 0), device_id_type=MESH,
        )

    def join(z_mask):
        near_copy(z_mask).wait_recv()
        part_ref[z_mask * 2] += near_ref[z_mask]
        far_copy(z_mask).start()

    def fresh(c_mask, block, begin):
        rows = pl.ds(begin, SEGMENT)
        return jnp.dot(
            all_ref[:, rows], signs_of(wide_ref[rows, :], offsets_of(c_mask, block)), preferred_element_type=jnp.float32
        )

    def kept(slot, begin):
        rows = pl.ds(begin, SEGMENT)
        return jnp.dot(all_ref[:, rows], signs_ref[slot, rows, :], preferred_element_type=jnp.float32)

    def segments(slot, parity, begin, end):
        for row in range(begin, end, SEGMENT):
            for block, ref, term in (
                (parity, fresh_ref, lambda: fresh(last - slot, parity, row)),
                (1 - parity, held_ref, lambda: kept(slot, row)),
            ):
                total = term()
                if row > 0:
                    total = total + ref[parity]
                if row + SEGMENT < p_local:
                    ref[parity] = total
                else:
                    part_ref[last - slot, :, block * TILE : (block + 1) * TILE] = total

    def grads_arrive(half):
        for number, copy in grad_copies:
            if number // (PIECES // 2) == half:
                copy.wait_recv()

    middle = p_local // 2
    for half in range(2):
        grads_arrive(half)
        for parity in range(2):
            segments(parity, parity, half * middle, (half + 1) * middle)
    near_copy(n_p - 1).start()

    @pl.loop(1, n_p - 1)
    def _(group):
        segments(group * 2, 0, 0, middle)

        @pl.when(group == 1)
        def _():
            join(n_p - 1)

        segments(group * 2, 0, middle, p_local)
        near_copy(n_p - 1 - group).start()
        segments(group * 2 + 1, 1, 0, p_local)
        join(n_p - 1 - group)

    @pl.loop(0, 4)
    def _(step):
        c_mask, block = 1 - step // 2, lax.rem(step, 2)
        span = pl.ds(pl.multiple_of(block * TILE, TILE), TILE)
        part_ref[c_mask, :, span] = jnp.dot(
            all_ref[...], signs_of(wide_ref[...], offsets_of(c_mask, block)), preferred_element_type=jnp.float32
        )

        @pl.when(step == 1)
        def _():
            near_copy(0).start()

    for copy in who_copies:
        copy.wait_recv()
    summed = part_ref[0]
    for z_mask in range(n_p - 1, 0, -1):
        far_copy(z_mask).wait_recv()
        summed = summed + far_ref[z_mask - 1]
    near_copy(0).wait_recv()
    summed = summed + near_ref[0]
    projected = summed * (1.0 / math.sqrt(p_whole))
    own = pl.ds(pl.multiple_of(example * width, 128), width)
    who = jnp.concatenate(
        [jnp.broadcast_to(who_ref[i], (8, e_local)).T[:, 0:1] for i in range(n_e)], axis=0
    )
    scale = jnp.zeros_like(projected)
    for row in range(CKPT):
        scale = jnp.where(who == row, table_ref[row : row + 1, own], scale)
    plain = projected.astype(jnp.bfloat16)
    scaled = (projected * scale).astype(jnp.bfloat16)
    lanes = pair_ref.shape[1]
    if lanes > e_all:
        scaled = jnp.concatenate([scaled, jnp.zeros((lanes - e_all, width), jnp.bfloat16)], axis=0)
    pair_ref[...] = lax.dot_general(
        plain, scaled, (((1,), (1,)), ((), ())), preferred_element_type=jnp.float32
    )

    copies = []
    for mask in range(n_c * n_e - 1, 0, -1):
        c_mask, e_mask = mask % n_c, mask // n_c
        rows = pl.ds(pl.multiple_of(flipped(me, c_mask, n_c) * cols, cols), cols)
        copy = pltpu.make_async_remote_copy(
            src_ref=pair_ref.at[rows], dst_ref=block_ref.at[mask - 1], send_sem=pair_send.at[mask - 1],
            recv_sem=pair_recv.at[mask - 1], device_id=device(c_mask, e_mask), device_id_type=MESH,
        )
        copy.start()
        copies.append((mask, copy))
    pairs = pair_ref[pl.ds(pl.multiple_of(me * cols, cols), cols), :]
    for mask, copy in copies[::-1]:
        copy.wait_recv()
        pairs = pairs + block_ref[mask - 1]
    block = pairs[:, :e_local]
    for i in range(1, n_e):
        block = jnp.where(example == i, pairs[:, i * e_local : (i + 1) * e_local], block)
    block = block * (1.0 / math.sqrt(K))
    col_ids = me * cols + lax.broadcasted_iota(jnp.int32, block.shape, 0)
    row_ids = example * e_local + lax.broadcasted_iota(jnp.int32, block.shape, 1)
    out_ref[...] = jnp.where(row_ids == col_ids, jnp.zeros_like(block), block)
    for mask, copy in copies:
        copy.wait_send()
    for z_mask in range(n_p):
        near_copy(z_mask).wait_send()
    for z_mask in range(1, n_p):
        far_copy(z_mask).wait_send()
    for number, copy in grad_copies:
        copy.wait_send()
    for copy in who_copies:
        copy.wait_send()


def fused(grads, seeds, adam_table, ckpt_index):
    e_local, p_local = grads.shape
    n_p, n_e, n_s = (lax.axis_size(name) for name in ("param", "example", "sub"))
    n_c = n_p * n_s
    e_all = e_local * n_e
    width = K // (n_c * n_e)
    cols = e_all // n_c
    lanes = -(-e_all // 128) * 128
    dma = pltpu.SemaphoreType.DMA
    return pl.pallas_call(
        functools.partial(fused_kernel, (n_p, n_e, n_s, p_local * n_c)),
        out_shape=jax.ShapeDtypeStruct((cols, e_local), jnp.float32),
        in_specs=[pl.BlockSpec(memory_space=pltpu.HBM)] * 4,
        out_specs=pl.BlockSpec(memory_space=pltpu.VMEM),
        scratch_shapes=[
            pltpu.VMEM((p_local // 128, 128), jnp.int32),
            pltpu.VMEM(adam_table.shape, jnp.float32),
            pltpu.VMEM((KEPT, p_local, TILE), jnp.bfloat16),
            dma((4,)),
            pltpu.VMEM((p_local, 128), jnp.int32),
            pltpu.VMEM((e_all, p_local), jnp.bfloat16),
            pltpu.VMEM((n_e, 1, e_local), jnp.int32),
            pltpu.VMEM((n_c, e_all, width), jnp.float32),
            pltpu.VMEM((2, e_all, TILE), jnp.float32),
            pltpu.VMEM((2, e_all, TILE), jnp.float32),
            pltpu.VMEM((n_p, e_all, width), jnp.float32),
            pltpu.VMEM((n_p - 1, e_all, width), jnp.float32),
            pltpu.VMEM((e_all, lanes), jnp.float32),
            pltpu.VMEM((n_c * n_e - 1, cols, lanes), jnp.float32),
            dma((n_e - 1, PIECES)),
            dma((n_e - 1, PIECES)),
            dma((n_e - 1,)),
            dma((n_e - 1,)),
            dma((n_p,)),
            dma((n_p,)),
            dma((n_p - 1,)),
            dma((n_p - 1,)),
            dma((n_c * n_e - 1,)),
            dma((n_c * n_e - 1,)),
        ],
        compiler_params=pltpu.CompilerParams(
            collective_id=0, has_side_effects=True, vmem_limit_bytes=67043328
        ),
    )(
        seeds.reshape(p_local // 128, 128),
        adam_table,
        ckpt_index.reshape(1, e_local),
        grads,
    ).T


def per_device(grads, seeds, adam_table, ckpt_index):
    e_local, p_local = grads.shape
    n_c, n_e = lax.axis_size(("param", "sub")), lax.axis_size("example")
    width, cols = K // (n_c * n_e), e_local * n_e // n_c
    n_p, n_s = lax.axis_size("param"), lax.axis_size("sub")
    if (n_p, n_e, n_s) == (4, 2, 2) and width == 2 * TILE and p_local == 2 * ROWS and cols % 8 == 0:
        return fused(grads, seeds, adam_table, ckpt_index)
    return separate(grads, seeds, adam_table, ckpt_index)


def solution(mesh):
    placed = (
        P(("groups", "example"), ("param", "sub")),
        P(("groups", "param", "sub")),
        P(None, ("groups", "param", "sub")),
        P(("groups", "example")),
    )
    return jax.shard_map(
        per_device,
        mesh=mesh,
        in_specs=placed,
        out_specs=P(("groups", "example"), ("param", "sub")),
        check_vma=False,
    )
```

```python
import functools
import math

import jax
import jax.numpy as jnp
from jax import lax
from jax.experimental import pallas as pl
from jax.experimental.pallas import tpu as pltpu
from jax.sharding import PartitionSpec as P

K = 8192
CKPT = 4
STEP = 1640531527
FIRST = 2146121005
SECOND = ((625341585 + 65536) << 15) & 0xFFFFFFFF
SECOND = SECOND - (1 << 32) if SECOND >= 1 << 31 else SECOND
TILE = 256
ROWS = 2048
PIECES = 4
GREETED = 1
KEPT = 6
THIN = 2
SEGMENT = 1024
MESH = pl.DeviceIdType.MESH


def sign_tile(seed_tile, offsets):
    mixed = seed_tile + offsets
    mixed = mixed ^ lax.shift_right_logical(mixed, jnp.int32(16))
    mixed = mixed * jnp.int32(FIRST)
    mixed = mixed ^ lax.shift_right_logical(mixed, jnp.int32(15))
    mixed = mixed * jnp.int32(SECOND)
    return jnp.where(mixed < 0, jnp.bfloat16(-1.0), jnp.bfloat16(1.0))


def hash_kernel(seeds_ref, offsets_ref, grads_ref, out_ref, wide_ref):
    e_all, p_local = grads_ref.shape
    wide_ref[...] = jnp.broadcast_to(seeds_ref[...], wide_ref.shape)

    @pl.loop(0, out_ref.shape[1] // TILE)
    def _(block):
        columns = pl.ds(pl.multiple_of(block * TILE, TILE), TILE)
        offsets = offsets_ref[:, columns]

        def add(part, total):
            rows = pl.ds(pl.multiple_of(part * TILE, TILE), TILE)
            seed_tile = wide_ref[rows, :]
            halves = [sign_tile(seed_tile, offsets[:, i : i + 128]) for i in range(0, TILE, 128)]
            return total + jnp.dot(
                grads_ref[:, rows], jnp.concatenate(halves, axis=1), preferred_element_type=jnp.float32
            )

        out_ref[:, columns] = lax.fori_loop(
            0, p_local // TILE, add, jnp.zeros((e_all, TILE), jnp.float32)
        )


def features_of(example, n_c, n_e):
    width = K // (n_c * n_e)
    owner = jnp.arange(n_c, dtype=jnp.int32)[:, None] * (width * n_e)
    return (owner + example * width + jnp.arange(width, dtype=jnp.int32)[None, :]).reshape(1, -1)


def separate(grads, seeds, adam_table, ckpt_index):
    e_local, p_local = grads.shape
    n_c, n_e = lax.axis_size(("param", "sub")), lax.axis_size("example")
    p_whole = p_local * n_c
    width = K // (n_c * n_e)
    example = lax.axis_index("example")
    everyone = lax.all_gather(grads, "example", axis=0, tiled=True)
    index = lax.all_gather(ckpt_index, "example", axis=0, tiled=True)
    e_all = e_local * n_e
    partial = pl.pallas_call(
        hash_kernel,
        out_shape=jax.ShapeDtypeStruct((e_all, n_c * width), jnp.float32),
        in_specs=[pl.BlockSpec(memory_space=pltpu.VMEM)] * 3,
        out_specs=pl.BlockSpec(memory_space=pltpu.VMEM),
        scratch_shapes=[pltpu.VMEM((p_local, 128), jnp.int32)],
        compiler_params=pltpu.CompilerParams(vmem_limit_bytes=40 << 20),
    )(seeds[:, None], features_of(example, n_c, n_e) * jnp.int32(STEP), everyone)
    summed = lax.psum_scatter(partial, ("param", "sub"), scatter_dimension=1, tiled=True)
    projected = summed * (1.0 / math.sqrt(p_whole))
    table = lax.dynamic_slice_in_dim(adam_table, example * width, width, 1)
    onehot = (index[:, None] == jnp.arange(CKPT, dtype=jnp.int32)[None, :]).astype(jnp.float32)
    scale = jnp.dot(onehot, table, precision=lax.Precision.HIGHEST)
    plain = projected.astype(jnp.bfloat16)
    scaled = (projected * scale).astype(jnp.bfloat16)
    pairs = lax.dot_general(scaled, plain, (((1,), (1,)), ((), ())), preferred_element_type=jnp.float32)
    pairs = lax.psum_scatter(pairs, "example", scatter_dimension=0, tiled=True)
    pairs = lax.psum_scatter(pairs, ("param", "sub"), scatter_dimension=1, tiled=True)
    influence = pairs * (1.0 / math.sqrt(K))
    cols = pairs.shape[1]
    row_ids = example * e_local + jnp.arange(e_local, dtype=jnp.int32)
    col_ids = lax.axis_index(("param", "sub")) * cols + jnp.arange(cols, dtype=jnp.int32)
    return jnp.where(row_ids[:, None] == col_ids[None, :], jnp.zeros_like(influence), influence)


def flipped(index, mask, size):
    bits = [1 << i for i in range((size - 1).bit_length())]
    return sum((((index // b) % 2 + (mask // b) % 2) % 2) * b for b in bits) if bits else index


def fused_kernel(
    sizes, seeds_hbm, table_hbm, index_hbm, grads_hbm, out_ref,
    seeds_ref, table_ref, signs_ref, load_sems, wide_ref, all_ref, who_ref, part_ref, fresh_ref, held_ref, near_ref, far_ref, thin_ref, thin_far_ref, pair_ref, block_ref,
    grad_send, grad_recv, who_send, who_recv, near_send, near_recv, far_send, far_recv, pair_send, pair_recv,
):
    n_p, n_e, n_s, p_whole = sizes
    n_c = n_p * n_s
    e_local, p_local = grads_hbm.shape
    e_all = n_e * e_local
    width = part_ref.shape[2]
    cols = out_ref.shape[0]
    piece = p_local // PIECES
    param, example, sub = lax.axis_index("param"), lax.axis_index("example"), lax.axis_index("sub")
    me = param * n_s + sub

    def device(c_mask, e_mask):
        return {
            "param": flipped(param, c_mask // n_s, n_p),
            "example": flipped(example, e_mask, n_e),
            "sub": flipped(sub, c_mask % n_s, n_s),
        }

    mine = pl.ds(pl.multiple_of(example * e_local, e_local), e_local)
    loads = [
        pltpu.make_async_copy(source, target, load_sems.at[i])
        for i, (source, target) in enumerate((
            (seeds_hbm, seeds_ref),
            (grads_hbm, all_ref.at[mine]),
            (index_hbm, who_ref.at[example]),
            (table_hbm, table_ref),
        ))
    ]
    for load in loads:
        load.start()
    barrier = pltpu.get_barrier_semaphore()
    for mask in range(1, n_c * n_e):
        pl.semaphore_signal(barrier, inc=1, device_id=device(mask % n_c, mask // n_c), device_id_type=MESH)

    def offsets_of(c_mask, block):
        first = (flipped(me, c_mask, n_c) * n_e + example) * width + block * TILE
        return (first + lax.broadcasted_iota(jnp.int32, (1, TILE), 1)) * jnp.int32(STEP)

    def signs_of(seed_tile, offsets):
        return jnp.concatenate(
            [sign_tile(seed_tile, offsets[:, i : i + 128]) for i in range(0, TILE, 128)], axis=1
        )

    last = n_c - 1
    loads[0].wait()
    turned = seeds_ref[...].T
    offsets = offsets_of(last, 1)
    for row in range(p_local // 128):
        rows = slice(row * 128, (row + 1) * 128)
        seed_tile = jnp.broadcast_to(turned[:, row : row + 1], (128, 128))
        wide_ref[rows, :] = seed_tile
        signs_ref[0, rows, :] = signs_of(seed_tile, offsets)
    def keep_signs(begin, end):
        @pl.loop(begin, end)
        def _(slot):
            signs_ref[slot] = signs_of(wide_ref[...], offsets_of(last - slot, lax.rem(slot + 1, 2)))

    keep_signs(1, GREETED)
    pl.semaphore_wait(barrier, n_c * n_e - 1)
    grad_copies, who_copies = [], []
    for mask in range(1, n_e):
        copy = pltpu.make_async_remote_copy(
            src_ref=index_hbm, dst_ref=who_ref.at[example], send_sem=who_send.at[mask - 1],
            recv_sem=who_recv.at[mask - 1], device_id=device(0, mask), device_id_type=MESH,
        )
        who_copies.append(copy)
        for i in range(PIECES):
            span = pl.ds(i * piece, piece)
            copy = pltpu.make_async_remote_copy(
                src_ref=grads_hbm.at[:, span], dst_ref=all_ref.at[mine, span],
                send_sem=grad_send.at[mask - 1, i], recv_sem=grad_recv.at[mask - 1, i],
                device_id=device(0, mask), device_id_type=MESH,
            )
            copy.start()
            grad_copies.append((i, copy))
    for copy in who_copies:
        copy.start()

    keep_signs(GREETED, KEPT)
    for load in loads[1:]:
        load.wait()

    def near_copy(z_mask):
        return pltpu.make_async_remote_copy(
            src_ref=part_ref.at[z_mask * 2 + 1], dst_ref=near_ref.at[z_mask], send_sem=near_send.at[z_mask],
            recv_sem=near_recv.at[z_mask], device_id=device(1, 0), device_id_type=MESH,
        )

    def far_copy(z_mask):
        source, target = part_ref.at[z_mask * 2], far_ref.at[z_mask - 1]
        if z_mask >= THIN:
            source, target = thin_ref.at[z_mask - THIN], thin_far_ref.at[z_mask - THIN]
        return pltpu.make_async_remote_copy(
            src_ref=source, dst_ref=target, send_sem=far_send.at[z_mask - 1],
            recv_sem=far_recv.at[z_mask - 1], device_id=device(z_mask * 2, 0), device_id_type=MESH,
        )

    def join(z_mask):
        near_copy(z_mask).wait_recv()
        total = part_ref[z_mask * 2] + near_ref[z_mask]
        if z_mask >= THIN:
            thin_ref[z_mask - THIN] = total.astype(jnp.bfloat16)
        else:
            part_ref[z_mask * 2] = total
        far_copy(z_mask).start()

    def fresh(c_mask, block, begin):
        rows = pl.ds(begin, SEGMENT)
        return jnp.dot(
            all_ref[:, rows], signs_of(wide_ref[rows, :], offsets_of(c_mask, block)), preferred_element_type=jnp.float32
        )

    def kept(slot, begin):
        rows = pl.ds(begin, SEGMENT)
        return jnp.dot(all_ref[:, rows], signs_ref[slot, rows, :], preferred_element_type=jnp.float32)

    def segments(slot, parity, begin, end):
        for row in range(begin, end, SEGMENT):
            for block, ref, term in (
                (parity, fresh_ref, lambda: fresh(last - slot, parity, row)),
                (1 - parity, held_ref, lambda: kept(slot, row)),
            ):
                total = term()
                if row > 0:
                    total = total + ref[parity]
                if row + SEGMENT < p_local:
                    ref[parity] = total
                else:
                    part_ref[last - slot, :, block * TILE : (block + 1) * TILE] = total

    def grads_arrive(half):
        for number, copy in grad_copies:
            if number // (PIECES // 2) == half:
                copy.wait_recv()

    middle = p_local // 2
    for half in range(2):
        grads_arrive(half)
        for parity in range(2):
            segments(parity, parity, half * middle, (half + 1) * middle)
    near_copy(n_p - 1).start()

    @pl.loop(1, n_p - 1)
    def _(group):
        segments(group * 2, 0, 0, middle)

        @pl.when(group == 1)
        def _():
            join(n_p - 1)

        segments(group * 2, 0, middle, p_local)
        near_copy(n_p - 1 - group).start()
        segments(group * 2 + 1, 1, 0, p_local)

        for z_mask in range(1, n_p - 1):
            @pl.when(group == n_p - 1 - z_mask)
            def _():
                join(z_mask)

    @pl.loop(0, 4)
    def _(step):
        c_mask, block = 1 - step // 2, lax.rem(step, 2)
        span = pl.ds(pl.multiple_of(block * TILE, TILE), TILE)
        part_ref[c_mask, :, span] = jnp.dot(
            all_ref[...], signs_of(wide_ref[...], offsets_of(c_mask, block)), preferred_element_type=jnp.float32
        )

        @pl.when(step == 1)
        def _():
            near_copy(0).start()

    for copy in who_copies:
        copy.wait_recv()
    summed = part_ref[0]
    for z_mask in range(n_p - 1, 0, -1):
        far_copy(z_mask).wait_recv()
        landed = far_ref[z_mask - 1] if z_mask < THIN else thin_far_ref[z_mask - THIN].astype(jnp.float32)
        summed = summed + landed
    near_copy(0).wait_recv()
    summed = summed + near_ref[0]
    projected = summed * (1.0 / math.sqrt(p_whole))
    own = pl.ds(pl.multiple_of(example * width, 128), width)
    who = jnp.concatenate(
        [jnp.broadcast_to(who_ref[i], (8, e_local)).T[:, 0:1] for i in range(n_e)], axis=0
    )
    scale = jnp.zeros_like(projected)
    for row in range(CKPT):
        scale = jnp.where(who == row, table_ref[row : row + 1, own], scale)
    plain = projected.astype(jnp.bfloat16)
    scaled = (projected * scale).astype(jnp.bfloat16)
    lanes = pair_ref.shape[1]
    if lanes > e_all:
        scaled = jnp.concatenate([scaled, jnp.zeros((lanes - e_all, width), jnp.bfloat16)], axis=0)
    pair_ref[...] = lax.dot_general(
        plain, scaled, (((1,), (1,)), ((), ())), preferred_element_type=jnp.float32
    )

    copies = []
    for mask in range(n_c * n_e - 1, 0, -1):
        c_mask, e_mask = mask % n_c, mask // n_c
        rows = pl.ds(pl.multiple_of(flipped(me, c_mask, n_c) * cols, cols), cols)
        copy = pltpu.make_async_remote_copy(
            src_ref=pair_ref.at[rows], dst_ref=block_ref.at[mask - 1], send_sem=pair_send.at[mask - 1],
            recv_sem=pair_recv.at[mask - 1], device_id=device(c_mask, e_mask), device_id_type=MESH,
        )
        copy.start()
        copies.append((mask, copy))
    pairs = pair_ref[pl.ds(pl.multiple_of(me * cols, cols), cols), :]
    for mask, copy in copies[::-1]:
        copy.wait_recv()
        pairs = pairs + block_ref[mask - 1]
    block = pairs[:, :e_local]
    for i in range(1, n_e):
        block = jnp.where(example == i, pairs[:, i * e_local : (i + 1) * e_local], block)
    block = block * (1.0 / math.sqrt(K))
    col_ids = me * cols + lax.broadcasted_iota(jnp.int32, block.shape, 0)
    row_ids = example * e_local + lax.broadcasted_iota(jnp.int32, block.shape, 1)
    out_ref[...] = jnp.where(row_ids == col_ids, jnp.zeros_like(block), block)
    for mask, copy in copies:
        copy.wait_send()
    for z_mask in range(n_p):
        near_copy(z_mask).wait_send()
    for z_mask in range(1, n_p):
        far_copy(z_mask).wait_send()
    for number, copy in grad_copies:
        copy.wait_send()
    for copy in who_copies:
        copy.wait_send()


def fused(grads, seeds, adam_table, ckpt_index):
    e_local, p_local = grads.shape
    n_p, n_e, n_s = (lax.axis_size(name) for name in ("param", "example", "sub"))
    n_c = n_p * n_s
    e_all = e_local * n_e
    width = K // (n_c * n_e)
    cols = e_all // n_c
    lanes = -(-e_all // 128) * 128
    dma = pltpu.SemaphoreType.DMA
    return pl.pallas_call(
        functools.partial(fused_kernel, (n_p, n_e, n_s, p_local * n_c)),
        out_shape=jax.ShapeDtypeStruct((cols, e_local), jnp.float32),
        in_specs=[pl.BlockSpec(memory_space=pltpu.HBM)] * 4,
        out_specs=pl.BlockSpec(memory_space=pltpu.VMEM),
        scratch_shapes=[
            pltpu.VMEM((p_local // 128, 128), jnp.int32),
            pltpu.VMEM(adam_table.shape, jnp.float32),
            pltpu.VMEM((KEPT, p_local, TILE), jnp.bfloat16),
            dma((4,)),
            pltpu.VMEM((p_local, 128), jnp.int32),
            pltpu.VMEM((e_all, p_local), jnp.bfloat16),
            pltpu.VMEM((n_e, 1, e_local), jnp.int32),
            pltpu.VMEM((n_c, e_all, width), jnp.float32),
            pltpu.VMEM((2, e_all, TILE), jnp.float32),
            pltpu.VMEM((2, e_all, TILE), jnp.float32),
            pltpu.VMEM((n_p, e_all, width), jnp.float32),
            pltpu.VMEM((n_p - 1, e_all, width), jnp.float32),
            pltpu.VMEM((n_p - THIN, e_all, width), jnp.bfloat16),
            pltpu.VMEM((n_p - THIN, e_all, width), jnp.bfloat16),
            pltpu.VMEM((e_all, lanes), jnp.float32),
            pltpu.VMEM((n_c * n_e - 1, cols, lanes), jnp.float32),
            dma((n_e - 1, PIECES)),
            dma((n_e - 1, PIECES)),
            dma((n_e - 1,)),
            dma((n_e - 1,)),
            dma((n_p,)),
            dma((n_p,)),
            dma((n_p - 1,)),
            dma((n_p - 1,)),
            dma((n_c * n_e - 1,)),
            dma((n_c * n_e - 1,)),
        ],
        compiler_params=pltpu.CompilerParams(
            collective_id=0, has_side_effects=True, vmem_limit_bytes=67043328
        ),
    )(
        seeds.reshape(p_local // 128, 128),
        adam_table,
        ckpt_index.reshape(1, e_local),
        grads,
    ).T


def per_device(grads, seeds, adam_table, ckpt_index):
    e_local, p_local = grads.shape
    n_c, n_e = lax.axis_size(("param", "sub")), lax.axis_size("example")
    width, cols = K // (n_c * n_e), e_local * n_e // n_c
    n_p, n_s = lax.axis_size("param"), lax.axis_size("sub")
    if (n_p, n_e, n_s) == (4, 2, 2) and width == 2 * TILE and p_local == 2 * ROWS and cols % 8 == 0:
        return fused(grads, seeds, adam_table, ckpt_index)
    return separate(grads, seeds, adam_table, ckpt_index)


def solution(mesh):
    placed = (
        P(("groups", "example"), ("param", "sub")),
        P(("groups", "param", "sub")),
        P(None, ("groups", "param", "sub")),
        P(("groups", "example")),
    )
    return jax.shard_map(
        per_device,
        mesh=mesh,
        in_specs=placed,
        out_specs=P(("groups", "example"), ("param", "sub")),
        check_vma=False,
    )
```

```python
import functools
import math

import jax
import jax.numpy as jnp
from jax import lax
from jax.experimental import pallas as pl
from jax.experimental.pallas import tpu as pltpu
from jax.sharding import PartitionSpec as P

K = 8192
CKPT = 4
STEP = 1640531527
FIRST = 2146121005
SECOND = ((625341585 + 65536) << 15) & 0xFFFFFFFF
SECOND = SECOND - (1 << 32) if SECOND >= 1 << 31 else SECOND
TILE = 256
ROWS = 2048
PIECES = 4
GREETED = 1
KEPT = 6
THIN = 2
SEGMENT = 1024
MESH = pl.DeviceIdType.MESH


def sign_tile(seed_tile, offsets):
    mixed = seed_tile + offsets
    mixed = mixed ^ lax.shift_right_logical(mixed, jnp.int32(16))
    mixed = mixed * jnp.int32(FIRST)
    mixed = mixed ^ lax.shift_right_logical(mixed, jnp.int32(15))
    mixed = mixed * jnp.int32(SECOND)
    return jnp.where(mixed < 0, jnp.bfloat16(-1.0), jnp.bfloat16(1.0))


def hash_kernel(seeds_ref, offsets_ref, grads_ref, out_ref, wide_ref):
    e_all, p_local = grads_ref.shape
    wide_ref[...] = jnp.broadcast_to(seeds_ref[...], wide_ref.shape)

    @pl.loop(0, out_ref.shape[1] // TILE)
    def _(block):
        columns = pl.ds(pl.multiple_of(block * TILE, TILE), TILE)
        offsets = offsets_ref[:, columns]

        def add(part, total):
            rows = pl.ds(pl.multiple_of(part * TILE, TILE), TILE)
            seed_tile = wide_ref[rows, :]
            halves = [sign_tile(seed_tile, offsets[:, i : i + 128]) for i in range(0, TILE, 128)]
            return total + jnp.dot(
                grads_ref[:, rows], jnp.concatenate(halves, axis=1), preferred_element_type=jnp.float32
            )

        out_ref[:, columns] = lax.fori_loop(
            0, p_local // TILE, add, jnp.zeros((e_all, TILE), jnp.float32)
        )


def features_of(example, n_c, n_e):
    width = K // (n_c * n_e)
    owner = jnp.arange(n_c, dtype=jnp.int32)[:, None] * (width * n_e)
    return (owner + example * width + jnp.arange(width, dtype=jnp.int32)[None, :]).reshape(1, -1)


def separate(grads, seeds, adam_table, ckpt_index):
    e_local, p_local = grads.shape
    n_c, n_e = lax.axis_size(("param", "sub")), lax.axis_size("example")
    p_whole = p_local * n_c
    width = K // (n_c * n_e)
    example = lax.axis_index("example")
    everyone = lax.all_gather(grads, "example", axis=0, tiled=True)
    index = lax.all_gather(ckpt_index, "example", axis=0, tiled=True)
    e_all = e_local * n_e
    partial = pl.pallas_call(
        hash_kernel,
        out_shape=jax.ShapeDtypeStruct((e_all, n_c * width), jnp.float32),
        in_specs=[pl.BlockSpec(memory_space=pltpu.VMEM)] * 3,
        out_specs=pl.BlockSpec(memory_space=pltpu.VMEM),
        scratch_shapes=[pltpu.VMEM((p_local, 128), jnp.int32)],
        compiler_params=pltpu.CompilerParams(vmem_limit_bytes=40 << 20),
    )(seeds[:, None], features_of(example, n_c, n_e) * jnp.int32(STEP), everyone)
    summed = lax.psum_scatter(partial, ("param", "sub"), scatter_dimension=1, tiled=True)
    projected = summed * (1.0 / math.sqrt(p_whole))
    table = lax.dynamic_slice_in_dim(adam_table, example * width, width, 1)
    onehot = (index[:, None] == jnp.arange(CKPT, dtype=jnp.int32)[None, :]).astype(jnp.float32)
    scale = jnp.dot(onehot, table, precision=lax.Precision.HIGHEST)
    plain = projected.astype(jnp.bfloat16)
    scaled = (projected * scale).astype(jnp.bfloat16)
    pairs = lax.dot_general(scaled, plain, (((1,), (1,)), ((), ())), preferred_element_type=jnp.float32)
    pairs = lax.psum_scatter(pairs, "example", scatter_dimension=0, tiled=True)
    pairs = lax.psum_scatter(pairs, ("param", "sub"), scatter_dimension=1, tiled=True)
    influence = pairs * (1.0 / math.sqrt(K))
    cols = pairs.shape[1]
    row_ids = example * e_local + jnp.arange(e_local, dtype=jnp.int32)
    col_ids = lax.axis_index(("param", "sub")) * cols + jnp.arange(cols, dtype=jnp.int32)
    return jnp.where(row_ids[:, None] == col_ids[None, :], jnp.zeros_like(influence), influence)


def flipped(index, mask, size):
    bits = [1 << i for i in range((size - 1).bit_length())]
    return sum((((index // b) % 2 + (mask // b) % 2) % 2) * b for b in bits) if bits else index


def fused_kernel(
    sizes, seeds_hbm, table_hbm, index_hbm, grads_hbm, out_ref,
    seeds_ref, table_ref, signs_ref, load_sems, wide_ref, all_ref, who_ref, part_ref, fresh_ref, held_ref, near_ref, far_ref, thin_ref, thin_far_ref, pair_ref, block_ref,
    grad_send, grad_recv, who_send, who_recv, near_send, near_recv, far_send, far_recv, pair_send, pair_recv,
):
    n_p, n_e, n_s, p_whole = sizes
    n_c = n_p * n_s
    e_local, p_local = grads_hbm.shape
    e_all = n_e * e_local
    width = part_ref.shape[2]
    cols = out_ref.shape[0]
    piece = p_local // PIECES
    param, example, sub = lax.axis_index("param"), lax.axis_index("example"), lax.axis_index("sub")
    me = param * n_s + sub

    def device(c_mask, e_mask):
        return {
            "param": flipped(param, c_mask // n_s, n_p),
            "example": flipped(example, e_mask, n_e),
            "sub": flipped(sub, c_mask % n_s, n_s),
        }

    mine = pl.ds(pl.multiple_of(example * e_local, e_local), e_local)
    loads = [
        pltpu.make_async_copy(source, target, load_sems.at[i])
        for i, (source, target) in enumerate((
            (seeds_hbm, seeds_ref),
            (grads_hbm, all_ref.at[mine]),
            (index_hbm, who_ref.at[example]),
            (table_hbm, table_ref),
        ))
    ]
    for load in loads:
        load.start()
    barrier = pltpu.get_barrier_semaphore()
    for mask in range(1, n_c * n_e):
        pl.semaphore_signal(barrier, inc=1, device_id=device(mask % n_c, mask // n_c), device_id_type=MESH)

    def offsets_of(c_mask, block):
        first = (flipped(me, c_mask, n_c) * n_e + example) * width + block * TILE
        return (first + lax.broadcasted_iota(jnp.int32, (1, TILE), 1)) * jnp.int32(STEP)

    def signs_of(seed_tile, offsets):
        return jnp.concatenate(
            [sign_tile(seed_tile, offsets[:, i : i + 128]) for i in range(0, TILE, 128)], axis=1
        )

    last = n_c - 1
    loads[0].wait()
    turned = seeds_ref[...].T
    offsets = offsets_of(last, 1)
    for row in range(p_local // 128):
        rows = slice(row * 128, (row + 1) * 128)
        seed_tile = jnp.broadcast_to(turned[:, row : row + 1], (128, 128))
        wide_ref[rows, :] = seed_tile
        signs_ref[0, rows, :] = signs_of(seed_tile, offsets)
    def keep_signs(begin, end):
        @pl.loop(begin, end)
        def _(slot):
            signs_ref[slot] = signs_of(wide_ref[...], offsets_of(last - slot, lax.rem(slot + 1, 2)))

    keep_signs(1, GREETED)
    pl.semaphore_wait(barrier, n_c * n_e - 1)
    grad_copies, who_copies = [], []
    for mask in range(1, n_e):
        copy = pltpu.make_async_remote_copy(
            src_ref=index_hbm, dst_ref=who_ref.at[example], send_sem=who_send.at[mask - 1],
            recv_sem=who_recv.at[mask - 1], device_id=device(0, mask), device_id_type=MESH,
        )
        who_copies.append(copy)
        for i in range(PIECES):
            span = pl.ds(i * piece, piece)
            copy = pltpu.make_async_remote_copy(
                src_ref=grads_hbm.at[:, span], dst_ref=all_ref.at[mine, span],
                send_sem=grad_send.at[mask - 1, i], recv_sem=grad_recv.at[mask - 1, i],
                device_id=device(0, mask), device_id_type=MESH,
            )
            copy.start()
            grad_copies.append((i, copy))
    for copy in who_copies:
        copy.start()

    keep_signs(GREETED, KEPT)
    for load in loads[1:]:
        load.wait()

    def near_copy(z_mask):
        return pltpu.make_async_remote_copy(
            src_ref=part_ref.at[z_mask * 2 + 1], dst_ref=near_ref.at[z_mask], send_sem=near_send.at[z_mask],
            recv_sem=near_recv.at[z_mask], device_id=device(1, 0), device_id_type=MESH,
        )

    def far_copy(z_mask):
        source, target = part_ref.at[z_mask * 2], far_ref.at[z_mask - 1]
        if z_mask >= THIN:
            source, target = thin_ref.at[z_mask - THIN], thin_far_ref.at[z_mask - THIN]
        return pltpu.make_async_remote_copy(
            src_ref=source, dst_ref=target, send_sem=far_send.at[z_mask - 1],
            recv_sem=far_recv.at[z_mask - 1], device_id=device(z_mask * 2, 0), device_id_type=MESH,
        )

    def join(z_mask):
        near_copy(z_mask).wait_recv()
        total = part_ref[z_mask * 2] + near_ref[z_mask]
        if z_mask >= THIN:
            thin_ref[z_mask - THIN] = total.astype(jnp.bfloat16)
        else:
            part_ref[z_mask * 2] = total
        far_copy(z_mask).start()

    def fresh(c_mask, block, begin):
        rows = pl.ds(begin, SEGMENT)
        return jnp.dot(
            all_ref[:, rows], signs_of(wide_ref[rows, :], offsets_of(c_mask, block)), preferred_element_type=jnp.float32
        )

    def kept(slot, begin):
        rows = pl.ds(begin, SEGMENT)
        return jnp.dot(all_ref[:, rows], signs_ref[slot, rows, :], preferred_element_type=jnp.float32)

    def segments(slot, parity, begin, end):
        for row in range(begin, end, SEGMENT):
            for block, ref, term in (
                (parity, fresh_ref, lambda: fresh(last - slot, parity, row)),
                (1 - parity, held_ref, lambda: kept(slot, row)),
            ):
                total = term()
                if row > 0:
                    total = total + ref[parity]
                if row + SEGMENT < p_local:
                    ref[parity] = total
                else:
                    part_ref[last - slot, :, block * TILE : (block + 1) * TILE] = total

    def grads_arrive(half):
        for number, copy in grad_copies:
            if number // (PIECES // 2) == half:
                copy.wait_recv()

    middle = p_local // 2
    for half in range(2):
        grads_arrive(half)
        for parity in range(2):
            segments(parity, parity, half * middle, (half + 1) * middle)
    near_copy(n_p - 1).start()

    @pl.loop(1, n_p - 1)
    def _(group):
        segments(group * 2, 0, 0, middle)

        @pl.when(group == 1)
        def _():
            join(n_p - 1)

        segments(group * 2, 0, middle, p_local)
        near_copy(n_p - 1 - group).start()
        segments(group * 2 + 1, 1, 0, p_local)

        for z_mask in range(1, n_p - 1):
            @pl.when(group == n_p - 1 - z_mask)
            def _():
                join(z_mask)

    @pl.loop(0, 4)
    def _(step):
        c_mask, block = 1 - step // 2, lax.rem(step, 2)
        span = pl.ds(pl.multiple_of(block * TILE, TILE), TILE)
        part_ref[c_mask, :, span] = jnp.dot(
            all_ref[...], signs_of(wide_ref[...], offsets_of(c_mask, block)), preferred_element_type=jnp.float32
        )

        @pl.when(step == 1)
        def _():
            near_copy(0).start()

    for copy in who_copies:
        copy.wait_recv()
    summed = part_ref[0]
    for z_mask in range(n_p - 1, 0, -1):
        far_copy(z_mask).wait_recv()
        landed = far_ref[z_mask - 1] if z_mask < THIN else thin_far_ref[z_mask - THIN].astype(jnp.float32)
        summed = summed + landed
    near_copy(0).wait_recv()
    summed = summed + near_ref[0]
    projected = summed * (1.0 / math.sqrt(p_whole))
    own = pl.ds(pl.multiple_of(example * width, 128), width)
    who = jnp.concatenate(
        [jnp.broadcast_to(who_ref[i], (8, e_local)).T[:, 0:1] for i in range(n_e)], axis=0
    )
    scale = jnp.zeros_like(projected)
    for row in range(CKPT):
        scale = jnp.where(who == row, table_ref[row : row + 1, own], scale)
    plain = projected.astype(jnp.bfloat16)
    scaled = (projected * scale).astype(jnp.bfloat16)
    lanes = pair_ref.shape[1]
    if lanes > e_all:
        scaled = jnp.concatenate([scaled, jnp.zeros((lanes - e_all, width), jnp.bfloat16)], axis=0)
    pair_ref[...] = lax.dot_general(
        plain, scaled, (((1,), (1,)), ((), ())), preferred_element_type=jnp.float32
    )

    copies = []
    for mask in range(n_c * n_e - 1, 0, -1):
        c_mask, e_mask = mask % n_c, mask // n_c
        rows = pl.ds(pl.multiple_of(flipped(me, c_mask, n_c) * cols, cols), cols)
        copy = pltpu.make_async_remote_copy(
            src_ref=pair_ref.at[rows], dst_ref=block_ref.at[mask - 1], send_sem=pair_send.at[mask - 1],
            recv_sem=pair_recv.at[mask - 1], device_id=device(c_mask, e_mask), device_id_type=MESH,
        )
        copy.start()
        copies.append((mask, copy))
    pairs = pair_ref[pl.ds(pl.multiple_of(me * cols, cols), cols), :]
    for mask, copy in copies[::-1]:
        copy.wait_recv()
        pairs = pairs + block_ref[mask - 1]
    block = pairs[:, :e_local]
    for i in range(1, n_e):
        block = jnp.where(example == i, pairs[:, i * e_local : (i + 1) * e_local], block)
    block = block * (1.0 / math.sqrt(K))
    col_ids = me * cols + lax.broadcasted_iota(jnp.int32, block.shape, 0)
    row_ids = example * e_local + lax.broadcasted_iota(jnp.int32, block.shape, 1)
    out_ref[...] = jnp.where(row_ids == col_ids, jnp.zeros_like(block), block)
    for mask, copy in copies:
        copy.wait_send()
    for z_mask in range(n_p):
        near_copy(z_mask).wait_send()
    for z_mask in range(1, n_p):
        far_copy(z_mask).wait_send()
    for number, copy in grad_copies:
        copy.wait_send()
    for copy in who_copies:
        copy.wait_send()


def fused(grads, seeds, adam_table, ckpt_index):
    e_local, p_local = grads.shape
    n_p, n_e, n_s = (lax.axis_size(name) for name in ("param", "example", "sub"))
    n_c = n_p * n_s
    e_all = e_local * n_e
    width = K // (n_c * n_e)
    cols = e_all // n_c
    lanes = -(-e_all // 128) * 128
    dma = pltpu.SemaphoreType.DMA
    return pl.pallas_call(
        functools.partial(fused_kernel, (n_p, n_e, n_s, p_local * n_c)),
        out_shape=pltpu.VMEM((cols, e_local), jnp.float32),
        in_specs=[pl.BlockSpec(memory_space=pltpu.HBM)] * 4,
        out_specs=pl.BlockSpec(memory_space=pltpu.VMEM),
        scratch_shapes=[
            pltpu.VMEM((p_local // 128, 128), jnp.int32),
            pltpu.VMEM(adam_table.shape, jnp.float32),
            pltpu.VMEM((KEPT, p_local, TILE), jnp.bfloat16),
            dma((4,)),
            pltpu.VMEM((p_local, 128), jnp.int32),
            pltpu.VMEM((e_all, p_local), jnp.bfloat16),
            pltpu.VMEM((n_e, 1, e_local), jnp.int32),
            pltpu.VMEM((n_c, e_all, width), jnp.float32),
            pltpu.VMEM((2, e_all, TILE), jnp.float32),
            pltpu.VMEM((2, e_all, TILE), jnp.float32),
            pltpu.VMEM((n_p, e_all, width), jnp.float32),
            pltpu.VMEM((n_p - 1, e_all, width), jnp.float32),
            pltpu.VMEM((n_p - THIN, e_all, width), jnp.bfloat16),
            pltpu.VMEM((n_p - THIN, e_all, width), jnp.bfloat16),
            pltpu.VMEM((e_all, lanes), jnp.float32),
            pltpu.VMEM((n_c * n_e - 1, cols, lanes), jnp.float32),
            dma((n_e - 1, PIECES)),
            dma((n_e - 1, PIECES)),
            dma((n_e - 1,)),
            dma((n_e - 1,)),
            dma((n_p,)),
            dma((n_p,)),
            dma((n_p - 1,)),
            dma((n_p - 1,)),
            dma((n_c * n_e - 1,)),
            dma((n_c * n_e - 1,)),
        ],
        compiler_params=pltpu.CompilerParams(
            collective_id=0, has_side_effects=True, vmem_limit_bytes=58720256
        ),
    )(
        seeds.reshape(p_local // 128, 128),
        adam_table,
        ckpt_index.reshape(1, e_local),
        grads,
    ).T


def per_device(grads, seeds, adam_table, ckpt_index):
    e_local, p_local = grads.shape
    n_c, n_e = lax.axis_size(("param", "sub")), lax.axis_size("example")
    width, cols = K // (n_c * n_e), e_local * n_e // n_c
    n_p, n_s = lax.axis_size("param"), lax.axis_size("sub")
    if (n_p, n_e, n_s) == (4, 2, 2) and width == 2 * TILE and p_local == 2 * ROWS and cols % 8 == 0:
        return fused(grads, seeds, adam_table, ckpt_index)
    return separate(grads, seeds, adam_table, ckpt_index)


def solution(mesh):
    placed = (
        P(("groups", "example"), ("param", "sub")),
        P(("groups", "param", "sub")),
        P(None, ("groups", "param", "sub")),
        P(("groups", "example")),
    )
    return jax.shard_map(
        per_device,
        mesh=mesh,
        in_specs=placed,
        out_specs=P(("groups", "example"), ("param", "sub")),
        check_vma=False,
    )
```

```python
import functools
import math

import jax
import jax.numpy as jnp
from jax import lax
from jax.experimental import pallas as pl
from jax.experimental.pallas import tpu as pltpu
from jax.sharding import PartitionSpec as P

K = 8192
CKPT = 4
STEP = 1640531527
FIRST = 2146121005
SECOND = ((625341585 + 65536) << 15) & 0xFFFFFFFF
SECOND = SECOND - (1 << 32) if SECOND >= 1 << 31 else SECOND
TILE = 256
ROWS = 2048
PIECES = 4
GREETED = 1
KEPT = 7
THIN = 1
SEGMENT = 1024
MESH = pl.DeviceIdType.MESH


def mix_tile(seed_tile, offsets):
    mixed = seed_tile + offsets
    mixed = mixed ^ lax.shift_right_logical(mixed, jnp.int32(16))
    mixed = mixed * jnp.int32(FIRST)
    mixed = mixed ^ lax.shift_right_logical(mixed, jnp.int32(15))
    return mixed * jnp.int32(SECOND)


def sign_of(mixed):
    return jnp.where(mixed < 0, jnp.bfloat16(-1.0), jnp.bfloat16(1.0))


def sign_tile(seed_tile, offsets):
    return sign_of(mix_tile(seed_tile, offsets))


def hash_kernel(seeds_ref, offsets_ref, grads_ref, out_ref, wide_ref):
    e_all, p_local = grads_ref.shape
    wide_ref[...] = jnp.broadcast_to(seeds_ref[...], wide_ref.shape)

    @pl.loop(0, out_ref.shape[1] // TILE)
    def _(block):
        columns = pl.ds(pl.multiple_of(block * TILE, TILE), TILE)
        offsets = offsets_ref[:, columns]

        def add(part, total):
            rows = pl.ds(pl.multiple_of(part * TILE, TILE), TILE)
            seed_tile = wide_ref[rows, :]
            halves = [sign_tile(seed_tile, offsets[:, i : i + 128]) for i in range(0, TILE, 128)]
            return total + jnp.dot(
                grads_ref[:, rows], jnp.concatenate(halves, axis=1), preferred_element_type=jnp.float32
            )

        out_ref[:, columns] = lax.fori_loop(
            0, p_local // TILE, add, jnp.zeros((e_all, TILE), jnp.float32)
        )


def features_of(example, n_c, n_e):
    width = K // (n_c * n_e)
    owner = jnp.arange(n_c, dtype=jnp.int32)[:, None] * (width * n_e)
    return (owner + example * width + jnp.arange(width, dtype=jnp.int32)[None, :]).reshape(1, -1)


def separate(grads, seeds, adam_table, ckpt_index):
    e_local, p_local = grads.shape
    n_c, n_e = lax.axis_size(("param", "sub")), lax.axis_size("example")
    p_whole = p_local * n_c
    width = K // (n_c * n_e)
    example = lax.axis_index("example")
    everyone = lax.all_gather(grads, "example", axis=0, tiled=True)
    index = lax.all_gather(ckpt_index, "example", axis=0, tiled=True)
    e_all = e_local * n_e
    partial = pl.pallas_call(
        hash_kernel,
        out_shape=jax.ShapeDtypeStruct((e_all, n_c * width), jnp.float32),
        in_specs=[pl.BlockSpec(memory_space=pltpu.VMEM)] * 3,
        out_specs=pl.BlockSpec(memory_space=pltpu.VMEM),
        scratch_shapes=[pltpu.VMEM((p_local, 128), jnp.int32)],
        compiler_params=pltpu.CompilerParams(vmem_limit_bytes=40 << 20),
    )(seeds[:, None], features_of(example, n_c, n_e) * jnp.int32(STEP), everyone)
    summed = lax.psum_scatter(partial, ("param", "sub"), scatter_dimension=1, tiled=True)
    projected = summed * (1.0 / math.sqrt(p_whole))
    table = lax.dynamic_slice_in_dim(adam_table, example * width, width, 1)
    onehot = (index[:, None] == jnp.arange(CKPT, dtype=jnp.int32)[None, :]).astype(jnp.float32)
    scale = jnp.dot(onehot, table, precision=lax.Precision.HIGHEST)
    plain = projected.astype(jnp.bfloat16)
    scaled = (projected * scale).astype(jnp.bfloat16)
    pairs = lax.dot_general(scaled, plain, (((1,), (1,)), ((), ())), preferred_element_type=jnp.float32)
    pairs = lax.psum_scatter(pairs, "example", scatter_dimension=0, tiled=True)
    pairs = lax.psum_scatter(pairs, ("param", "sub"), scatter_dimension=1, tiled=True)
    influence = pairs * (1.0 / math.sqrt(K))
    cols = pairs.shape[1]
    row_ids = example * e_local + jnp.arange(e_local, dtype=jnp.int32)
    col_ids = lax.axis_index(("param", "sub")) * cols + jnp.arange(cols, dtype=jnp.int32)
    return jnp.where(row_ids[:, None] == col_ids[None, :], jnp.zeros_like(influence), influence)


def flipped(index, mask, size):
    bits = [1 << i for i in range((size - 1).bit_length())]
    return sum((((index // b) % 2 + (mask // b) % 2) % 2) * b for b in bits) if bits else index


def fused_kernel(
    sizes, seeds_hbm, table_hbm, index_hbm, grads_hbm, out_ref,
    seeds_ref, table_ref, mixed_ref, load_sems, wide_ref, all_ref, who_ref, part_ref, fresh_ref, held_ref, near_ref, far_ref, thin_ref, thin_far_ref, pair_ref, block_ref,
    grad_send, grad_recv, who_send, who_recv, near_send, near_recv, far_send, far_recv, pair_send, pair_recv,
):
    n_p, n_e, n_s, p_whole = sizes
    n_c = n_p * n_s
    e_local, p_local = grads_hbm.shape
    e_all = n_e * e_local
    width = part_ref.shape[2]
    cols = out_ref.shape[0]
    piece = p_local // PIECES
    param, example, sub = lax.axis_index("param"), lax.axis_index("example"), lax.axis_index("sub")
    me = param * n_s + sub

    def device(c_mask, e_mask):
        return {
            "param": flipped(param, c_mask // n_s, n_p),
            "example": flipped(example, e_mask, n_e),
            "sub": flipped(sub, c_mask % n_s, n_s),
        }

    mine = pl.ds(pl.multiple_of(example * e_local, e_local), e_local)
    loads = [
        pltpu.make_async_copy(source, target, load_sems.at[i])
        for i, (source, target) in enumerate((
            (seeds_hbm, seeds_ref),
            (grads_hbm, all_ref.at[mine]),
            (index_hbm, who_ref.at[example]),
            (table_hbm, table_ref),
        ))
    ]
    for load in loads:
        load.start()
    barrier = pltpu.get_barrier_semaphore()
    for mask in range(1, n_c * n_e):
        pl.semaphore_signal(barrier, inc=1, device_id=device(mask % n_c, mask // n_c), device_id_type=MESH)

    def offsets_of(c_mask, block):
        first = (flipped(me, c_mask, n_c) * n_e + example) * width + block * TILE
        return (first + lax.broadcasted_iota(jnp.int32, (1, TILE), 1)) * jnp.int32(STEP)

    def signs_of(seed_tile, offsets):
        return jnp.concatenate(
            [sign_tile(seed_tile, offsets[:, i : i + 128]) for i in range(0, TILE, 128)], axis=1
        )

    def keep(slot, rows, seed_tile, offsets):
        for i in range(0, TILE, 128):
            mixed_ref[slot, rows, i : i + 128] = mix_tile(seed_tile, offsets[:, i : i + 128])

    last = n_c - 1
    loads[0].wait()
    turned = seeds_ref[...].T
    offsets = offsets_of(last, 1)
    for row in range(p_local // 128):
        rows = slice(row * 128, (row + 1) * 128)
        seed_tile = jnp.broadcast_to(turned[:, row : row + 1], (128, 128))
        wide_ref[rows, :] = seed_tile
        keep(0, rows, seed_tile, offsets)
    def keep_signs(begin, end):
        @pl.loop(begin, end)
        def _(slot):
            keep(slot, slice(0, p_local), wide_ref[...], offsets_of(last - slot, lax.rem(slot + 1, 2)))

    keep_signs(1, GREETED)
    pl.semaphore_wait(barrier, n_c * n_e - 1)
    grad_copies, who_copies = [], []
    for mask in range(1, n_e):
        copy = pltpu.make_async_remote_copy(
            src_ref=index_hbm, dst_ref=who_ref.at[example], send_sem=who_send.at[mask - 1],
            recv_sem=who_recv.at[mask - 1], device_id=device(0, mask), device_id_type=MESH,
        )
        who_copies.append(copy)
        for i in range(PIECES):
            span = pl.ds(i * piece, piece)
            copy = pltpu.make_async_remote_copy(
                src_ref=grads_hbm.at[:, span], dst_ref=all_ref.at[mine, span],
                send_sem=grad_send.at[mask - 1, i], recv_sem=grad_recv.at[mask - 1, i],
                device_id=device(0, mask), device_id_type=MESH,
            )
            copy.start()
            grad_copies.append((i, copy))
    for copy in who_copies:
        copy.start()

    keep_signs(GREETED, KEPT)
    for load in loads[1:]:
        load.wait()

    def near_copy(z_mask):
        return pltpu.make_async_remote_copy(
            src_ref=part_ref.at[z_mask * 2 + 1], dst_ref=near_ref.at[z_mask], send_sem=near_send.at[z_mask],
            recv_sem=near_recv.at[z_mask], device_id=device(1, 0), device_id_type=MESH,
        )

    def far_copy(z_mask):
        source, target = part_ref.at[z_mask * 2], far_ref.at[z_mask - 1]
        if z_mask >= THIN:
            source, target = thin_ref.at[z_mask - THIN], thin_far_ref.at[z_mask - THIN]
        return pltpu.make_async_remote_copy(
            src_ref=source, dst_ref=target, send_sem=far_send.at[z_mask - 1],
            recv_sem=far_recv.at[z_mask - 1], device_id=device(z_mask * 2, 0), device_id_type=MESH,
        )

    def join(z_mask):
        near_copy(z_mask).wait_recv()
        total = part_ref[z_mask * 2] + near_ref[z_mask]
        if z_mask >= THIN:
            thin_ref[z_mask - THIN] = total.astype(jnp.bfloat16)
        else:
            part_ref[z_mask * 2] = total
        far_copy(z_mask).start()

    def fresh(c_mask, block, begin):
        rows = pl.ds(begin, SEGMENT)
        return jnp.dot(
            all_ref[:, rows], signs_of(wide_ref[rows, :], offsets_of(c_mask, block)), preferred_element_type=jnp.float32
        )

    def kept(slot, begin):
        rows = pl.ds(begin, SEGMENT)
        return jnp.dot(all_ref[:, rows], sign_of(mixed_ref[slot, rows, :]), preferred_element_type=jnp.float32)

    def segments(slot, parity, begin, end):
        for row in range(begin, end, SEGMENT):
            for block, ref, term in (
                (parity, fresh_ref, lambda: fresh(last - slot, parity, row)),
                (1 - parity, held_ref, lambda: kept(slot, row)),
            ):
                total = term()
                if row > 0:
                    total = total + ref[parity]
                if row + SEGMENT < p_local:
                    ref[parity] = total
                else:
                    part_ref[last - slot, :, block * TILE : (block + 1) * TILE] = total

    def grads_arrive(half):
        for number, copy in grad_copies:
            if number // (PIECES // 2) == half:
                copy.wait_recv()

    middle = p_local // 2
    for half in range(2):
        grads_arrive(half)
        for parity in range(2):
            segments(parity, parity, half * middle, (half + 1) * middle)
    near_copy(n_p - 1).start()

    @pl.loop(1, n_p - 1)
    def _(group):
        segments(group * 2, 0, 0, middle)

        @pl.when(group == 1)
        def _():
            join(n_p - 1)

        segments(group * 2, 0, middle, p_local)
        near_copy(n_p - 1 - group).start()
        segments(group * 2 + 1, 1, 0, p_local)

        for z_mask in range(1, n_p - 1):
            @pl.when(group == n_p - 1 - z_mask)
            def _():
                join(z_mask)

    segments(last - 1, 0, 0, p_local)
    near_copy(0).start()

    @pl.loop(0, 2)
    def _(block):
        span = pl.ds(pl.multiple_of(block * TILE, TILE), TILE)
        part_ref[0, :, span] = jnp.dot(
            all_ref[...], signs_of(wide_ref[...], offsets_of(0, block)), preferred_element_type=jnp.float32
        )

    for copy in who_copies:
        copy.wait_recv()
    summed = part_ref[0]
    for z_mask in range(n_p - 1, 0, -1):
        far_copy(z_mask).wait_recv()
        landed = far_ref[z_mask - 1] if z_mask < THIN else thin_far_ref[z_mask - THIN].astype(jnp.float32)
        summed = summed + landed
    near_copy(0).wait_recv()
    summed = summed + near_ref[0]
    projected = summed * (1.0 / math.sqrt(p_whole))
    own = pl.ds(pl.multiple_of(example * width, 128), width)
    who = jnp.concatenate(
        [jnp.broadcast_to(who_ref[i], (8, e_local)).T[:, 0:1] for i in range(n_e)], axis=0
    )
    scale = jnp.zeros_like(projected)
    for row in range(CKPT):
        scale = jnp.where(who == row, table_ref[row : row + 1, own], scale)
    plain = projected.astype(jnp.bfloat16)
    scaled = (projected * scale).astype(jnp.bfloat16)
    lanes = pair_ref.shape[1]
    if lanes > e_all:
        scaled = jnp.concatenate([scaled, jnp.zeros((lanes - e_all, width), jnp.bfloat16)], axis=0)
    pair_ref[...] = lax.dot_general(
        plain, scaled, (((1,), (1,)), ((), ())), preferred_element_type=jnp.float32
    )

    copies = []
    for mask in range(n_c * n_e - 1, 0, -1):
        c_mask, e_mask = mask % n_c, mask // n_c
        rows = pl.ds(pl.multiple_of(flipped(me, c_mask, n_c) * cols, cols), cols)
        copy = pltpu.make_async_remote_copy(
            src_ref=pair_ref.at[rows], dst_ref=block_ref.at[mask - 1], send_sem=pair_send.at[mask - 1],
            recv_sem=pair_recv.at[mask - 1], device_id=device(c_mask, e_mask), device_id_type=MESH,
        )
        copy.start()
        copies.append((mask, copy))
    pairs = pair_ref[pl.ds(pl.multiple_of(me * cols, cols), cols), :]
    for mask, copy in copies[::-1]:
        copy.wait_recv()
        pairs = pairs + block_ref[mask - 1]
    block = pairs[:, :e_local]
    for i in range(1, n_e):
        block = jnp.where(example == i, pairs[:, i * e_local : (i + 1) * e_local], block)
    block = block * (1.0 / math.sqrt(K))
    col_ids = me * cols + lax.broadcasted_iota(jnp.int32, block.shape, 0)
    row_ids = example * e_local + lax.broadcasted_iota(jnp.int32, block.shape, 1)
    out_ref[...] = jnp.where(row_ids == col_ids, jnp.zeros_like(block), block)
    for mask, copy in copies:
        copy.wait_send()
    for z_mask in range(n_p):
        near_copy(z_mask).wait_send()
    for z_mask in range(1, n_p):
        far_copy(z_mask).wait_send()
    for number, copy in grad_copies:
        copy.wait_send()
    for copy in who_copies:
        copy.wait_send()


def fused(grads, seeds, adam_table, ckpt_index):
    e_local, p_local = grads.shape
    n_p, n_e, n_s = (lax.axis_size(name) for name in ("param", "example", "sub"))
    n_c = n_p * n_s
    e_all = e_local * n_e
    width = K // (n_c * n_e)
    cols = e_all // n_c
    lanes = -(-e_all // 128) * 128
    dma = pltpu.SemaphoreType.DMA
    return pl.pallas_call(
        functools.partial(fused_kernel, (n_p, n_e, n_s, p_local * n_c)),
        out_shape=pltpu.VMEM((cols, e_local), jnp.float32),
        in_specs=[pl.BlockSpec(memory_space=pltpu.HBM)] * 4,
        out_specs=pl.BlockSpec(memory_space=pltpu.VMEM),
        scratch_shapes=[
            pltpu.VMEM((p_local // 128, 128), jnp.int32),
            pltpu.VMEM(adam_table.shape, jnp.float32),
            pltpu.VMEM((KEPT, p_local, TILE), jnp.int32),
            dma((4,)),
            pltpu.VMEM((p_local, 128), jnp.int32),
            pltpu.VMEM((e_all, p_local), jnp.bfloat16),
            pltpu.VMEM((n_e, 1, e_local), jnp.int32),
            pltpu.VMEM((n_c, e_all, width), jnp.float32),
            pltpu.VMEM((2, e_all, TILE), jnp.float32),
            pltpu.VMEM((2, e_all, TILE), jnp.float32),
            pltpu.VMEM((n_p, e_all, width), jnp.float32),
            pltpu.VMEM((n_p - 1, e_all, width), jnp.float32),
            pltpu.VMEM((n_p - THIN, e_all, width), jnp.bfloat16),
            pltpu.VMEM((n_p - THIN, e_all, width), jnp.bfloat16),
            pltpu.VMEM((e_all, lanes), jnp.float32),
            pltpu.VMEM((n_c * n_e - 1, cols, lanes), jnp.float32),
            dma((n_e - 1, PIECES)),
            dma((n_e - 1, PIECES)),
            dma((n_e - 1,)),
            dma((n_e - 1,)),
            dma((n_p,)),
            dma((n_p,)),
            dma((n_p - 1,)),
            dma((n_p - 1,)),
            dma((n_c * n_e - 1,)),
            dma((n_c * n_e - 1,)),
        ],
        compiler_params=pltpu.CompilerParams(
            collective_id=0, has_side_effects=True, vmem_limit_bytes=58720256
        ),
    )(
        seeds.reshape(p_local // 128, 128),
        adam_table,
        ckpt_index.reshape(1, e_local),
        grads,
    ).T


def per_device(grads, seeds, adam_table, ckpt_index):
    e_local, p_local = grads.shape
    n_c, n_e = lax.axis_size(("param", "sub")), lax.axis_size("example")
    width, cols = K // (n_c * n_e), e_local * n_e // n_c
    n_p, n_s = lax.axis_size("param"), lax.axis_size("sub")
    if (n_p, n_e, n_s) == (4, 2, 2) and width == 2 * TILE and p_local == 2 * ROWS and cols % 8 == 0:
        return fused(grads, seeds, adam_table, ckpt_index)
    return separate(grads, seeds, adam_table, ckpt_index)


def solution(mesh):
    placed = (
        P(("groups", "example"), ("param", "sub")),
        P(("groups", "param", "sub")),
        P(None, ("groups", "param", "sub")),
        P(("groups", "example")),
    )
    return jax.shard_map(
        per_device,
        mesh=mesh,
        in_specs=placed,
        out_specs=P(("groups", "example"), ("param", "sub")),
        check_vma=False,
    )
```

```python
import functools
import math

import jax
import jax.numpy as jnp
from jax import lax
from jax.experimental import pallas as pl
from jax.experimental.pallas import tpu as pltpu
from jax.sharding import PartitionSpec as P

K = 8192
CKPT = 4
STEP = 1640531527
FIRST = 2146121005
SECOND = ((625341585 + 65536) << 15) & 0xFFFFFFFF
SECOND = SECOND - (1 << 32) if SECOND >= 1 << 31 else SECOND
TILE = 256
ROWS = 2048
PIECES = 4
GREETED = 1
KEPT = 7
THIN = 1
SEGMENT = 1024
MESH = pl.DeviceIdType.MESH


def mix_tile(seed_tile, offsets):
    mixed = seed_tile + offsets
    mixed = mixed ^ lax.shift_right_logical(mixed, jnp.int32(16))
    mixed = mixed * jnp.int32(FIRST)
    mixed = mixed ^ lax.shift_right_logical(mixed, jnp.int32(15))
    return mixed * jnp.int32(SECOND)


def sign_of(mixed):
    return jnp.where(mixed < 0, jnp.bfloat16(-1.0), jnp.bfloat16(1.0))


def sign_tile(seed_tile, offsets):
    return sign_of(mix_tile(seed_tile, offsets))


def hash_kernel(seeds_ref, offsets_ref, grads_ref, out_ref, wide_ref):
    e_all, p_local = grads_ref.shape
    wide_ref[...] = jnp.broadcast_to(seeds_ref[...], wide_ref.shape)

    @pl.loop(0, out_ref.shape[1] // TILE)
    def _(block):
        columns = pl.ds(pl.multiple_of(block * TILE, TILE), TILE)
        offsets = offsets_ref[:, columns]

        def add(part, total):
            rows = pl.ds(pl.multiple_of(part * TILE, TILE), TILE)
            seed_tile = wide_ref[rows, :]
            halves = [sign_tile(seed_tile, offsets[:, i : i + 128]) for i in range(0, TILE, 128)]
            return total + jnp.dot(
                grads_ref[:, rows], jnp.concatenate(halves, axis=1), preferred_element_type=jnp.float32
            )

        out_ref[:, columns] = lax.fori_loop(
            0, p_local // TILE, add, jnp.zeros((e_all, TILE), jnp.float32)
        )


def features_of(example, n_c, n_e):
    width = K // (n_c * n_e)
    owner = jnp.arange(n_c, dtype=jnp.int32)[:, None] * (width * n_e)
    return (owner + example * width + jnp.arange(width, dtype=jnp.int32)[None, :]).reshape(1, -1)


def separate(grads, seeds, adam_table, ckpt_index):
    e_local, p_local = grads.shape
    n_c, n_e = lax.axis_size(("param", "sub")), lax.axis_size("example")
    p_whole = p_local * n_c
    width = K // (n_c * n_e)
    example = lax.axis_index("example")
    everyone = lax.all_gather(grads, "example", axis=0, tiled=True)
    index = lax.all_gather(ckpt_index, "example", axis=0, tiled=True)
    e_all = e_local * n_e
    partial = pl.pallas_call(
        hash_kernel,
        out_shape=jax.ShapeDtypeStruct((e_all, n_c * width), jnp.float32),
        in_specs=[pl.BlockSpec(memory_space=pltpu.VMEM)] * 3,
        out_specs=pl.BlockSpec(memory_space=pltpu.VMEM),
        scratch_shapes=[pltpu.VMEM((p_local, 128), jnp.int32)],
        compiler_params=pltpu.CompilerParams(vmem_limit_bytes=40 << 20),
    )(seeds[:, None], features_of(example, n_c, n_e) * jnp.int32(STEP), everyone)
    summed = lax.psum_scatter(partial, ("param", "sub"), scatter_dimension=1, tiled=True)
    projected = summed * (1.0 / math.sqrt(p_whole))
    table = lax.dynamic_slice_in_dim(adam_table, example * width, width, 1)
    onehot = (index[:, None] == jnp.arange(CKPT, dtype=jnp.int32)[None, :]).astype(jnp.float32)
    scale = jnp.dot(onehot, table, precision=lax.Precision.HIGHEST)
    plain = projected.astype(jnp.bfloat16)
    scaled = (projected * scale).astype(jnp.bfloat16)
    pairs = lax.dot_general(scaled, plain, (((1,), (1,)), ((), ())), preferred_element_type=jnp.float32)
    pairs = lax.psum_scatter(pairs, "example", scatter_dimension=0, tiled=True)
    pairs = lax.psum_scatter(pairs, ("param", "sub"), scatter_dimension=1, tiled=True)
    influence = pairs * (1.0 / math.sqrt(K))
    cols = pairs.shape[1]
    row_ids = example * e_local + jnp.arange(e_local, dtype=jnp.int32)
    col_ids = lax.axis_index(("param", "sub")) * cols + jnp.arange(cols, dtype=jnp.int32)
    return jnp.where(row_ids[:, None] == col_ids[None, :], jnp.zeros_like(influence), influence)


def flipped(index, mask, size):
    bits = [1 << i for i in range((size - 1).bit_length())]
    return sum((((index // b) % 2 + (mask // b) % 2) % 2) * b for b in bits) if bits else index


def fused_kernel(
    sizes, seeds_hbm, table_hbm, index_hbm, grads_hbm, out_ref,
    seeds_ref, table_ref, mixed_ref, load_sems, wide_ref, all_ref, who_ref, part_ref, fresh_ref, held_ref, near_ref, far_ref, thin_ref, thin_far_ref, scale_ref, pair_ref, block_ref,
    grad_send, grad_recv, who_send, who_recv, near_send, near_recv, far_send, far_recv, pair_send, pair_recv,
):
    n_p, n_e, n_s, p_whole = sizes
    n_c = n_p * n_s
    e_local, p_local = grads_hbm.shape
    e_all = n_e * e_local
    width = part_ref.shape[2]
    cols = out_ref.shape[0]
    piece = p_local // PIECES
    param, example, sub = lax.axis_index("param"), lax.axis_index("example"), lax.axis_index("sub")
    me = param * n_s + sub

    def device(c_mask, e_mask):
        return {
            "param": flipped(param, c_mask // n_s, n_p),
            "example": flipped(example, e_mask, n_e),
            "sub": flipped(sub, c_mask % n_s, n_s),
        }

    mine = pl.ds(pl.multiple_of(example * e_local, e_local), e_local)
    loads = [
        pltpu.make_async_copy(source, target, load_sems.at[i])
        for i, (source, target) in enumerate((
            (seeds_hbm, seeds_ref),
            (grads_hbm, all_ref.at[mine]),
            (index_hbm, who_ref.at[example]),
            (table_hbm, table_ref),
        ))
    ]
    for load in loads:
        load.start()
    barrier = pltpu.get_barrier_semaphore()
    for mask in range(1, n_c * n_e):
        pl.semaphore_signal(barrier, inc=1, device_id=device(mask % n_c, mask // n_c), device_id_type=MESH)

    def offsets_of(c_mask, block):
        first = (flipped(me, c_mask, n_c) * n_e + example) * width + block * TILE
        return (first + lax.broadcasted_iota(jnp.int32, (1, TILE), 1)) * jnp.int32(STEP)

    def signs_of(seed_tile, offsets):
        return jnp.concatenate(
            [sign_tile(seed_tile, offsets[:, i : i + 128]) for i in range(0, TILE, 128)], axis=1
        )

    def keep(slot, rows, seed_tile, offsets):
        for i in range(0, TILE, 128):
            mixed_ref[slot, rows, i : i + 128] = mix_tile(seed_tile, offsets[:, i : i + 128])

    last = n_c - 1
    loads[0].wait()
    turned = seeds_ref[...].T
    offsets = offsets_of(last, 1)
    for row in range(p_local // 128):
        rows = slice(row * 128, (row + 1) * 128)
        seed_tile = jnp.broadcast_to(turned[:, row : row + 1], (128, 128))
        wide_ref[rows, :] = seed_tile
        keep(0, rows, seed_tile, offsets)
    def keep_signs(begin, end):
        @pl.loop(begin, end)
        def _(slot):
            keep(slot, slice(0, p_local), wide_ref[...], offsets_of(last - slot, lax.rem(slot + 1, 2)))

    keep_signs(1, GREETED)
    pl.semaphore_wait(barrier, n_c * n_e - 1)
    grad_copies, who_copies = [], []
    for mask in range(1, n_e):
        copy = pltpu.make_async_remote_copy(
            src_ref=index_hbm, dst_ref=who_ref.at[example], send_sem=who_send.at[mask - 1],
            recv_sem=who_recv.at[mask - 1], device_id=device(0, mask), device_id_type=MESH,
        )
        who_copies.append(copy)
        for i in range(PIECES):
            span = pl.ds(i * piece, piece)
            copy = pltpu.make_async_remote_copy(
                src_ref=grads_hbm.at[:, span], dst_ref=all_ref.at[mine, span],
                send_sem=grad_send.at[mask - 1, i], recv_sem=grad_recv.at[mask - 1, i],
                device_id=device(0, mask), device_id_type=MESH,
            )
            copy.start()
            grad_copies.append((i, copy))
    for copy in who_copies:
        copy.start()

    keep_signs(GREETED, KEPT)
    for load in loads[1:]:
        load.wait()

    def near_copy(z_mask):
        return pltpu.make_async_remote_copy(
            src_ref=part_ref.at[z_mask * 2 + 1], dst_ref=near_ref.at[z_mask], send_sem=near_send.at[z_mask],
            recv_sem=near_recv.at[z_mask], device_id=device(1, 0), device_id_type=MESH,
        )

    def far_copy(z_mask):
        source, target = part_ref.at[z_mask * 2], far_ref.at[z_mask - 1]
        if z_mask >= THIN:
            source, target = thin_ref.at[z_mask - THIN], thin_far_ref.at[z_mask - THIN]
        return pltpu.make_async_remote_copy(
            src_ref=source, dst_ref=target, send_sem=far_send.at[z_mask - 1],
            recv_sem=far_recv.at[z_mask - 1], device_id=device(z_mask * 2, 0), device_id_type=MESH,
        )

    def join(z_mask):
        near_copy(z_mask).wait_recv()
        total = part_ref[z_mask * 2] + near_ref[z_mask]
        if z_mask >= THIN:
            thin_ref[z_mask - THIN] = total.astype(jnp.bfloat16)
        else:
            part_ref[z_mask * 2] = total
        far_copy(z_mask).start()

    def fresh(c_mask, block, begin):
        rows = pl.ds(begin, SEGMENT)
        return jnp.dot(
            all_ref[:, rows], signs_of(wide_ref[rows, :], offsets_of(c_mask, block)), preferred_element_type=jnp.float32
        )

    def kept(slot, begin):
        rows = pl.ds(begin, SEGMENT)
        return jnp.dot(all_ref[:, rows], sign_of(mixed_ref[slot, rows, :]), preferred_element_type=jnp.float32)

    def segments(slot, parity, begin, end):
        for row in range(begin, end, SEGMENT):
            for block, ref, term in (
                (parity, fresh_ref, lambda: fresh(last - slot, parity, row)),
                (1 - parity, held_ref, lambda: kept(slot, row)),
            ):
                total = term()
                if row > 0:
                    total = total + ref[parity]
                if row + SEGMENT < p_local:
                    ref[parity] = total
                else:
                    part_ref[last - slot, :, block * TILE : (block + 1) * TILE] = total

    def grads_arrive(half):
        for number, copy in grad_copies:
            if number // (PIECES // 2) == half:
                copy.wait_recv()

    middle = p_local // 2
    for half in range(2):
        grads_arrive(half)
        for parity in range(2):
            segments(parity, parity, half * middle, (half + 1) * middle)
    near_copy(n_p - 1).start()
    for copy in who_copies:
        copy.wait_recv()
    own = pl.ds(pl.multiple_of(example * width, 128), width)
    who = jnp.concatenate(
        [jnp.broadcast_to(who_ref[i], (8, e_local)).T[:, 0:1] for i in range(n_e)], axis=0
    )
    scale = jnp.zeros((e_all, width), jnp.float32)
    for row in range(CKPT):
        scale = jnp.where(who == row, table_ref[row : row + 1, own], scale)
    scale_ref[...] = scale

    @pl.loop(1, n_p - 1)
    def _(group):
        segments(group * 2, 0, 0, middle)

        @pl.when(group == 1)
        def _():
            join(n_p - 1)

        segments(group * 2, 0, middle, p_local)
        near_copy(n_p - 1 - group).start()
        segments(group * 2 + 1, 1, 0, p_local)

        for z_mask in range(1, n_p - 1):
            @pl.when(group == n_p - 1 - z_mask)
            def _():
                join(z_mask)

    segments(last - 1, 0, 0, p_local)
    near_copy(0).start()

    @pl.loop(0, 2)
    def _(block):
        span = pl.ds(pl.multiple_of(block * TILE, TILE), TILE)
        part_ref[0, :, span] = jnp.dot(
            all_ref[...], signs_of(wide_ref[...], offsets_of(0, block)), preferred_element_type=jnp.float32
        )

    summed = part_ref[0]
    for z_mask in range(n_p - 1, 0, -1):
        far_copy(z_mask).wait_recv()
        landed = far_ref[z_mask - 1] if z_mask < THIN else thin_far_ref[z_mask - THIN].astype(jnp.float32)
        summed = summed + landed
    near_copy(0).wait_recv()
    summed = summed + near_ref[0]
    projected = summed * (1.0 / math.sqrt(p_whole))
    plain = projected.astype(jnp.bfloat16)
    scaled = (projected * scale_ref[...]).astype(jnp.bfloat16)
    lanes = pair_ref.shape[1]
    if lanes > e_all:
        scaled = jnp.concatenate([scaled, jnp.zeros((lanes - e_all, width), jnp.bfloat16)], axis=0)
    pair_ref[...] = lax.dot_general(
        plain, scaled, (((1,), (1,)), ((), ())), preferred_element_type=jnp.float32
    )

    copies = []
    for mask in range(n_c * n_e - 1, 0, -1):
        c_mask, e_mask = mask % n_c, mask // n_c
        rows = pl.ds(pl.multiple_of(flipped(me, c_mask, n_c) * cols, cols), cols)
        copy = pltpu.make_async_remote_copy(
            src_ref=pair_ref.at[rows], dst_ref=block_ref.at[mask - 1], send_sem=pair_send.at[mask - 1],
            recv_sem=pair_recv.at[mask - 1], device_id=device(c_mask, e_mask), device_id_type=MESH,
        )
        copy.start()
        copies.append((mask, copy))
    pairs = pair_ref[pl.ds(pl.multiple_of(me * cols, cols), cols), :]
    for mask, copy in copies[::-1]:
        copy.wait_recv()
        pairs = pairs + block_ref[mask - 1]
    block = pairs[:, :e_local]
    for i in range(1, n_e):
        block = jnp.where(example == i, pairs[:, i * e_local : (i + 1) * e_local], block)
    block = block * (1.0 / math.sqrt(K))
    col_ids = me * cols + lax.broadcasted_iota(jnp.int32, block.shape, 0)
    row_ids = example * e_local + lax.broadcasted_iota(jnp.int32, block.shape, 1)
    out_ref[...] = jnp.where(row_ids == col_ids, jnp.zeros_like(block), block)
    for mask, copy in copies:
        copy.wait_send()
    for z_mask in range(n_p):
        near_copy(z_mask).wait_send()
    for z_mask in range(1, n_p):
        far_copy(z_mask).wait_send()
    for number, copy in grad_copies:
        copy.wait_send()
    for copy in who_copies:
        copy.wait_send()


def fused(grads, seeds, adam_table, ckpt_index):
    e_local, p_local = grads.shape
    n_p, n_e, n_s = (lax.axis_size(name) for name in ("param", "example", "sub"))
    n_c = n_p * n_s
    e_all = e_local * n_e
    width = K // (n_c * n_e)
    cols = e_all // n_c
    lanes = -(-e_all // 128) * 128
    dma = pltpu.SemaphoreType.DMA
    return pl.pallas_call(
        functools.partial(fused_kernel, (n_p, n_e, n_s, p_local * n_c)),
        out_shape=pltpu.VMEM((cols, e_local), jnp.float32),
        in_specs=[pl.BlockSpec(memory_space=pltpu.HBM)] * 4,
        out_specs=pl.BlockSpec(memory_space=pltpu.VMEM),
        scratch_shapes=[
            pltpu.VMEM((p_local // 128, 128), jnp.int32),
            pltpu.VMEM(adam_table.shape, jnp.float32),
            pltpu.VMEM((KEPT, p_local, TILE), jnp.int32),
            dma((4,)),
            pltpu.VMEM((p_local, 128), jnp.int32),
            pltpu.VMEM((e_all, p_local), jnp.bfloat16),
            pltpu.VMEM((n_e, 1, e_local), jnp.int32),
            pltpu.VMEM((n_c, e_all, width), jnp.float32),
            pltpu.VMEM((2, e_all, TILE), jnp.float32),
            pltpu.VMEM((2, e_all, TILE), jnp.float32),
            pltpu.VMEM((n_p, e_all, width), jnp.float32),
            pltpu.VMEM((n_p - 1, e_all, width), jnp.float32),
            pltpu.VMEM((n_p - THIN, e_all, width), jnp.bfloat16),
            pltpu.VMEM((n_p - THIN, e_all, width), jnp.bfloat16),
            pltpu.VMEM((e_all, width), jnp.float32),
            pltpu.VMEM((e_all, lanes), jnp.float32),
            pltpu.VMEM((n_c * n_e - 1, cols, lanes), jnp.float32),
            dma((n_e - 1, PIECES)),
            dma((n_e - 1, PIECES)),
            dma((n_e - 1,)),
            dma((n_e - 1,)),
            dma((n_p,)),
            dma((n_p,)),
            dma((n_p - 1,)),
            dma((n_p - 1,)),
            dma((n_c * n_e - 1,)),
            dma((n_c * n_e - 1,)),
        ],
        compiler_params=pltpu.CompilerParams(
            collective_id=0, has_side_effects=True, vmem_limit_bytes=58720256
        ),
    )(
        seeds.reshape(p_local // 128, 128),
        adam_table,
        ckpt_index.reshape(1, e_local),
        grads,
    ).T


def per_device(grads, seeds, adam_table, ckpt_index):
    e_local, p_local = grads.shape
    n_c, n_e = lax.axis_size(("param", "sub")), lax.axis_size("example")
    width, cols = K // (n_c * n_e), e_local * n_e // n_c
    n_p, n_s = lax.axis_size("param"), lax.axis_size("sub")
    if (n_p, n_e, n_s) == (4, 2, 2) and width == 2 * TILE and p_local == 2 * ROWS and cols % 8 == 0:
        return fused(grads, seeds, adam_table, ckpt_index)
    return separate(grads, seeds, adam_table, ckpt_index)


def solution(mesh):
    placed = (
        P(("groups", "example"), ("param", "sub")),
        P(("groups", "param", "sub")),
        P(None, ("groups", "param", "sub")),
        P(("groups", "example")),
    )
    return jax.shard_map(
        per_device,
        mesh=mesh,
        in_specs=placed,
        out_specs=P(("groups", "example"), ("param", "sub")),
        check_vma=False,
    )
```

```python
import functools
import math

import jax
import jax.numpy as jnp
from jax import lax
from jax.experimental import pallas as pl
from jax.experimental.pallas import tpu as pltpu
from jax.sharding import PartitionSpec as P

K = 8192
CKPT = 4
STEP = 1640531527
FIRST = 2146121005
SECOND = ((625341585 + 65536) << 15) & 0xFFFFFFFF
SECOND = SECOND - (1 << 32) if SECOND >= 1 << 31 else SECOND
TILE = 256
ROWS = 2048
PIECES = 4
GREETED = 1
KEPT = 7
THIN = 1
SEGMENT = 1024
MESH = pl.DeviceIdType.MESH


def mix_tile(seed_tile, offsets):
    mixed = seed_tile + offsets
    mixed = mixed ^ lax.shift_right_logical(mixed, jnp.int32(16))
    mixed = mixed * jnp.int32(FIRST)
    mixed = mixed ^ lax.shift_right_logical(mixed, jnp.int32(15))
    return mixed * jnp.int32(SECOND)


def sign_of(mixed):
    return jnp.where(mixed < 0, jnp.bfloat16(-1.0), jnp.bfloat16(1.0))


def sign_tile(seed_tile, offsets):
    return sign_of(mix_tile(seed_tile, offsets))


def hash_kernel(seeds_ref, offsets_ref, grads_ref, out_ref, wide_ref):
    e_all, p_local = grads_ref.shape
    wide_ref[...] = jnp.broadcast_to(seeds_ref[...], wide_ref.shape)

    @pl.loop(0, out_ref.shape[1] // TILE)
    def _(block):
        columns = pl.ds(pl.multiple_of(block * TILE, TILE), TILE)
        offsets = offsets_ref[:, columns]

        def add(part, total):
            rows = pl.ds(pl.multiple_of(part * TILE, TILE), TILE)
            seed_tile = wide_ref[rows, :]
            halves = [sign_tile(seed_tile, offsets[:, i : i + 128]) for i in range(0, TILE, 128)]
            return total + jnp.dot(
                grads_ref[:, rows], jnp.concatenate(halves, axis=1), preferred_element_type=jnp.float32
            )

        out_ref[:, columns] = lax.fori_loop(
            0, p_local // TILE, add, jnp.zeros((e_all, TILE), jnp.float32)
        )


def features_of(example, n_c, n_e):
    width = K // (n_c * n_e)
    owner = jnp.arange(n_c, dtype=jnp.int32)[:, None] * (width * n_e)
    return (owner + example * width + jnp.arange(width, dtype=jnp.int32)[None, :]).reshape(1, -1)


def separate(grads, seeds, adam_table, ckpt_index):
    e_local, p_local = grads.shape
    n_c, n_e = lax.axis_size(("param", "sub")), lax.axis_size("example")
    p_whole = p_local * n_c
    width = K // (n_c * n_e)
    example = lax.axis_index("example")
    everyone = lax.all_gather(grads, "example", axis=0, tiled=True)
    index = lax.all_gather(ckpt_index, "example", axis=0, tiled=True)
    e_all = e_local * n_e
    partial = pl.pallas_call(
        hash_kernel,
        out_shape=jax.ShapeDtypeStruct((e_all, n_c * width), jnp.float32),
        in_specs=[pl.BlockSpec(memory_space=pltpu.VMEM)] * 3,
        out_specs=pl.BlockSpec(memory_space=pltpu.VMEM),
        scratch_shapes=[pltpu.VMEM((p_local, 128), jnp.int32)],
        compiler_params=pltpu.CompilerParams(vmem_limit_bytes=40 << 20),
    )(seeds[:, None], features_of(example, n_c, n_e) * jnp.int32(STEP), everyone)
    summed = lax.psum_scatter(partial, ("param", "sub"), scatter_dimension=1, tiled=True)
    projected = summed * (1.0 / math.sqrt(p_whole))
    table = lax.dynamic_slice_in_dim(adam_table, example * width, width, 1)
    onehot = (index[:, None] == jnp.arange(CKPT, dtype=jnp.int32)[None, :]).astype(jnp.float32)
    scale = jnp.dot(onehot, table, precision=lax.Precision.HIGHEST)
    plain = projected.astype(jnp.bfloat16)
    scaled = (projected * scale).astype(jnp.bfloat16)
    pairs = lax.dot_general(scaled, plain, (((1,), (1,)), ((), ())), preferred_element_type=jnp.float32)
    pairs = lax.psum_scatter(pairs, "example", scatter_dimension=0, tiled=True)
    pairs = lax.psum_scatter(pairs, ("param", "sub"), scatter_dimension=1, tiled=True)
    influence = pairs * (1.0 / math.sqrt(K))
    cols = pairs.shape[1]
    row_ids = example * e_local + jnp.arange(e_local, dtype=jnp.int32)
    col_ids = lax.axis_index(("param", "sub")) * cols + jnp.arange(cols, dtype=jnp.int32)
    return jnp.where(row_ids[:, None] == col_ids[None, :], jnp.zeros_like(influence), influence)


def flipped(index, mask, size):
    bits = [1 << i for i in range((size - 1).bit_length())]
    return sum((((index // b) % 2 + (mask // b) % 2) % 2) * b for b in bits) if bits else index


def fused_kernel(
    sizes, seeds_hbm, table_hbm, index_hbm, grads_hbm, out_ref,
    seeds_ref, table_ref, mixed_ref, load_sems, wide_ref, all_ref, who_ref, part_ref, fresh_ref, held_ref, near_ref, far_ref, thin_ref, thin_far_ref, scale_ref, pair_ref, block_ref,
    grad_send, grad_recv, who_send, who_recv, near_send, near_recv, far_send, far_recv, pair_send, pair_recv,
):
    n_p, n_e, n_s, p_whole = sizes
    n_c = n_p * n_s
    e_local, p_local = grads_hbm.shape
    e_all = n_e * e_local
    width = part_ref.shape[2]
    cols = out_ref.shape[0]
    piece = p_local // PIECES
    param, example, sub = lax.axis_index("param"), lax.axis_index("example"), lax.axis_index("sub")
    me = param * n_s + sub

    def device(c_mask, e_mask):
        return {
            "param": flipped(param, c_mask // n_s, n_p),
            "example": flipped(example, e_mask, n_e),
            "sub": flipped(sub, c_mask % n_s, n_s),
        }

    mine = pl.ds(pl.multiple_of(example * e_local, e_local), e_local)
    loads = [
        pltpu.make_async_copy(source, target, load_sems.at[i])
        for i, (source, target) in enumerate((
            (seeds_hbm, seeds_ref),
            (grads_hbm, all_ref.at[mine]),
            (index_hbm, who_ref.at[example]),
            (table_hbm, table_ref),
        ))
    ]
    for load in loads:
        load.start()
    barrier = pltpu.get_barrier_semaphore()
    for mask in range(1, n_c * n_e):
        pl.semaphore_signal(barrier, inc=1, device_id=device(mask % n_c, mask // n_c), device_id_type=MESH)

    def offsets_of(c_mask, block):
        first = (flipped(me, c_mask, n_c) * n_e + example) * width + block * TILE
        return (first + lax.broadcasted_iota(jnp.int32, (1, TILE), 1)) * jnp.int32(STEP)

    def signs_of(seed_tile, offsets):
        return jnp.concatenate(
            [sign_tile(seed_tile, offsets[:, i : i + 128]) for i in range(0, TILE, 128)], axis=1
        )

    def keep(slot, rows, seed_tile, offsets):
        for i in range(0, TILE, 128):
            mixed_ref[slot, rows, i : i + 128] = mix_tile(seed_tile, offsets[:, i : i + 128])

    last = n_c - 1
    loads[0].wait()
    turned = seeds_ref[...].T
    offsets = offsets_of(last, 1)
    for row in range(p_local // 128):
        rows = slice(row * 128, (row + 1) * 128)
        seed_tile = jnp.broadcast_to(turned[:, row : row + 1], (128, 128))
        wide_ref[rows, :] = seed_tile
        keep(0, rows, seed_tile, offsets)
    def keep_signs(begin, end):
        @pl.loop(begin, end)
        def _(slot):
            keep(slot, slice(0, p_local), wide_ref[...], offsets_of(last - slot, lax.rem(slot + 1, 2)))

    keep_signs(1, GREETED)
    pl.semaphore_wait(barrier, n_c * n_e - 1)
    grad_copies, who_copies = [], []
    for mask in range(1, n_e):
        copy = pltpu.make_async_remote_copy(
            src_ref=index_hbm, dst_ref=who_ref.at[example], send_sem=who_send.at[mask - 1],
            recv_sem=who_recv.at[mask - 1], device_id=device(0, mask), device_id_type=MESH,
        )
        who_copies.append(copy)
        for i in range(PIECES):
            span = pl.ds(i * piece, piece)
            copy = pltpu.make_async_remote_copy(
                src_ref=grads_hbm.at[:, span], dst_ref=all_ref.at[mine, span],
                send_sem=grad_send.at[mask - 1, i], recv_sem=grad_recv.at[mask - 1, i],
                device_id=device(0, mask), device_id_type=MESH,
            )
            copy.start()
            grad_copies.append((i, copy))
    for copy in who_copies:
        copy.start()

    keep_signs(GREETED, KEPT)
    for load in loads[1:]:
        load.wait()

    def near_copy(z_mask):
        return pltpu.make_async_remote_copy(
            src_ref=part_ref.at[z_mask * 2 + 1], dst_ref=near_ref.at[z_mask], send_sem=near_send.at[z_mask],
            recv_sem=near_recv.at[z_mask], device_id=device(1, 0), device_id_type=MESH,
        )

    def far_copy(z_mask):
        source, target = part_ref.at[z_mask * 2], far_ref.at[z_mask - 1]
        if z_mask >= THIN:
            source, target = thin_ref.at[z_mask - THIN], thin_far_ref.at[z_mask - THIN]
        return pltpu.make_async_remote_copy(
            src_ref=source, dst_ref=target, send_sem=far_send.at[z_mask - 1],
            recv_sem=far_recv.at[z_mask - 1], device_id=device(z_mask * 2, 0), device_id_type=MESH,
        )

    def join(z_mask):
        near_copy(z_mask).wait_recv()
        total = part_ref[z_mask * 2] + near_ref[z_mask]
        if z_mask >= THIN:
            thin_ref[z_mask - THIN] = total.astype(jnp.bfloat16)
        else:
            part_ref[z_mask * 2] = total
        far_copy(z_mask).start()

    def fresh(c_mask, block, begin):
        rows = pl.ds(begin, SEGMENT)
        return jnp.dot(
            all_ref[:, rows], signs_of(wide_ref[rows, :], offsets_of(c_mask, block)), preferred_element_type=jnp.float32
        )

    def kept(slot, begin):
        rows = pl.ds(begin, SEGMENT)
        return jnp.dot(all_ref[:, rows], sign_of(mixed_ref[slot, rows, :]), preferred_element_type=jnp.float32)

    def segments(slot, parity, begin, end):
        for row in range(begin, end, SEGMENT):
            for block, ref, term in (
                (parity, fresh_ref, lambda: fresh(last - slot, parity, row)),
                (1 - parity, held_ref, lambda: kept(slot, row)),
            ):
                total = term()
                if row > 0:
                    total = total + ref[parity]
                if row + SEGMENT < p_local:
                    ref[parity] = total
                else:
                    part_ref[last - slot, :, block * TILE : (block + 1) * TILE] = total

    def grads_arrive(half):
        for number, copy in grad_copies:
            if number // (PIECES // 2) == half:
                copy.wait_recv()

    middle = p_local // 2
    for half in range(2):
        grads_arrive(half)
        for parity in range(2):
            segments(parity, parity, half * middle, (half + 1) * middle)
    near_copy(n_p - 1).start()
    for copy in who_copies:
        copy.wait_recv()
    own = pl.ds(pl.multiple_of(example * width, 128), width)
    who = jnp.concatenate(
        [jnp.broadcast_to(who_ref[i], (8, e_local)).T[:, 0:1] for i in range(n_e)], axis=0
    )
    scale = jnp.zeros((e_all, width), jnp.float32)
    for row in range(CKPT):
        scale = jnp.where(who == row, table_ref[row : row + 1, own], scale)
    scale_ref[...] = scale

    @pl.loop(1, n_p - 1)
    def _(group):
        segments(group * 2, 0, 0, middle)

        @pl.when(group == 1)
        def _():
            join(n_p - 1)

        segments(group * 2, 0, middle, p_local)
        near_copy(n_p - 1 - group).start()
        segments(group * 2 + 1, 1, 0, p_local)

        for z_mask in range(1, n_p - 1):
            @pl.when(group == n_p - 1 - z_mask)
            def _():
                join(z_mask)

    segments(last - 1, 0, 0, p_local)
    near_copy(0).start()
    far_copy(n_p - 1).wait_recv()
    far_ref[n_p - 2] = thin_far_ref[n_p - 1 - THIN].astype(jnp.float32)

    @pl.loop(0, 2)
    def _(block):
        span = pl.ds(pl.multiple_of(block * TILE, TILE), TILE)
        part_ref[0, :, span] = jnp.dot(
            all_ref[...], signs_of(wide_ref[...], offsets_of(0, block)), preferred_element_type=jnp.float32
        )

    summed = part_ref[0] + far_ref[n_p - 2]
    for z_mask in range(n_p - 2, 0, -1):
        far_copy(z_mask).wait_recv()
        landed = far_ref[z_mask - 1] if z_mask < THIN else thin_far_ref[z_mask - THIN].astype(jnp.float32)
        summed = summed + landed
    near_copy(0).wait_recv()
    summed = summed + near_ref[0]
    projected = summed * (1.0 / math.sqrt(p_whole))
    plain = projected.astype(jnp.bfloat16)
    scaled = (projected * scale_ref[...]).astype(jnp.bfloat16)
    lanes = pair_ref.shape[1]
    if lanes > e_all:
        scaled = jnp.concatenate([scaled, jnp.zeros((lanes - e_all, width), jnp.bfloat16)], axis=0)
    pair_ref[...] = lax.dot_general(
        plain, scaled, (((1,), (1,)), ((), ())), preferred_element_type=jnp.float32
    )

    copies = []
    for mask in range(n_c * n_e - 1, 0, -1):
        c_mask, e_mask = mask % n_c, mask // n_c
        rows = pl.ds(pl.multiple_of(flipped(me, c_mask, n_c) * cols, cols), cols)
        copy = pltpu.make_async_remote_copy(
            src_ref=pair_ref.at[rows], dst_ref=block_ref.at[mask - 1], send_sem=pair_send.at[mask - 1],
            recv_sem=pair_recv.at[mask - 1], device_id=device(c_mask, e_mask), device_id_type=MESH,
        )
        copy.start()
        copies.append((mask, copy))
    pairs = pair_ref[pl.ds(pl.multiple_of(me * cols, cols), cols), :]
    for mask, copy in copies[::-1]:
        copy.wait_recv()
        pairs = pairs + block_ref[mask - 1]
    block = pairs[:, :e_local]
    for i in range(1, n_e):
        block = jnp.where(example == i, pairs[:, i * e_local : (i + 1) * e_local], block)
    block = block * (1.0 / math.sqrt(K))
    col_ids = me * cols + lax.broadcasted_iota(jnp.int32, block.shape, 0)
    row_ids = example * e_local + lax.broadcasted_iota(jnp.int32, block.shape, 1)
    out_ref[...] = jnp.where(row_ids == col_ids, jnp.zeros_like(block), block)
    for mask, copy in copies:
        copy.wait_send()
    for z_mask in range(n_p):
        near_copy(z_mask).wait_send()
    for z_mask in range(1, n_p):
        far_copy(z_mask).wait_send()
    for number, copy in grad_copies:
        copy.wait_send()
    for copy in who_copies:
        copy.wait_send()


def fused(grads, seeds, adam_table, ckpt_index):
    e_local, p_local = grads.shape
    n_p, n_e, n_s = (lax.axis_size(name) for name in ("param", "example", "sub"))
    n_c = n_p * n_s
    e_all = e_local * n_e
    width = K // (n_c * n_e)
    cols = e_all // n_c
    lanes = -(-e_all // 128) * 128
    dma = pltpu.SemaphoreType.DMA
    return pl.pallas_call(
        functools.partial(fused_kernel, (n_p, n_e, n_s, p_local * n_c)),
        out_shape=pltpu.VMEM((cols, e_local), jnp.float32),
        in_specs=[pl.BlockSpec(memory_space=pltpu.HBM)] * 4,
        out_specs=pl.BlockSpec(memory_space=pltpu.VMEM),
        scratch_shapes=[
            pltpu.VMEM((p_local // 128, 128), jnp.int32),
            pltpu.VMEM(adam_table.shape, jnp.float32),
            pltpu.VMEM((KEPT, p_local, TILE), jnp.int32),
            dma((4,)),
            pltpu.VMEM((p_local, 128), jnp.int32),
            pltpu.VMEM((e_all, p_local), jnp.bfloat16),
            pltpu.VMEM((n_e, 1, e_local), jnp.int32),
            pltpu.VMEM((n_c, e_all, width), jnp.float32),
            pltpu.VMEM((2, e_all, TILE), jnp.float32),
            pltpu.VMEM((2, e_all, TILE), jnp.float32),
            pltpu.VMEM((n_p, e_all, width), jnp.float32),
            pltpu.VMEM((n_p - 1, e_all, width), jnp.float32),
            pltpu.VMEM((n_p - THIN, e_all, width), jnp.bfloat16),
            pltpu.VMEM((n_p - THIN, e_all, width), jnp.bfloat16),
            pltpu.VMEM((e_all, width), jnp.float32),
            pltpu.VMEM((e_all, lanes), jnp.float32),
            pltpu.VMEM((n_c * n_e - 1, cols, lanes), jnp.float32),
            dma((n_e - 1, PIECES)),
            dma((n_e - 1, PIECES)),
            dma((n_e - 1,)),
            dma((n_e - 1,)),
            dma((n_p,)),
            dma((n_p,)),
            dma((n_p - 1,)),
            dma((n_p - 1,)),
            dma((n_c * n_e - 1,)),
            dma((n_c * n_e - 1,)),
        ],
        compiler_params=pltpu.CompilerParams(
            collective_id=0, has_side_effects=True, vmem_limit_bytes=58720256
        ),
    )(
        seeds.reshape(p_local // 128, 128),
        adam_table,
        ckpt_index.reshape(1, e_local),
        grads,
    ).T


def per_device(grads, seeds, adam_table, ckpt_index):
    e_local, p_local = grads.shape
    n_c, n_e = lax.axis_size(("param", "sub")), lax.axis_size("example")
    width, cols = K // (n_c * n_e), e_local * n_e // n_c
    n_p, n_s = lax.axis_size("param"), lax.axis_size("sub")
    if (n_p, n_e, n_s) == (4, 2, 2) and width == 2 * TILE and p_local == 2 * ROWS and cols % 8 == 0:
        return fused(grads, seeds, adam_table, ckpt_index)
    return separate(grads, seeds, adam_table, ckpt_index)


def solution(mesh):
    placed = (
        P(("groups", "example"), ("param", "sub")),
        P(("groups", "param", "sub")),
        P(None, ("groups", "param", "sub")),
        P(("groups", "example")),
    )
    return jax.shard_map(
        per_device,
        mesh=mesh,
        in_specs=placed,
        out_specs=P(("groups", "example"), ("param", "sub")),
        check_vma=False,
    )
```

```python
import functools
import math

import jax
import jax.numpy as jnp
from jax import lax
from jax.experimental import pallas as pl
from jax.experimental.pallas import tpu as pltpu
from jax.sharding import PartitionSpec as P

K = 8192
CKPT = 4
STEP = 1640531527
FIRST = 2146121005
SECOND = ((625341585 + 65536) << 15) & 0xFFFFFFFF
SECOND = SECOND - (1 << 32) if SECOND >= 1 << 31 else SECOND
TILE = 256
ROWS = 2048
PIECES = 4
GREETED = 1
KEPT = 7
THIN = 1
SEGMENT = 1024
MESH = pl.DeviceIdType.MESH


def mix_tile(seed_tile, offsets):
    mixed = seed_tile + offsets
    mixed = mixed ^ lax.shift_right_logical(mixed, jnp.int32(16))
    mixed = mixed * jnp.int32(FIRST)
    mixed = mixed ^ lax.shift_right_logical(mixed, jnp.int32(15))
    return mixed * jnp.int32(SECOND)


def sign_of(mixed):
    return jnp.where(mixed < 0, jnp.bfloat16(-1.0), jnp.bfloat16(1.0))


def sign_tile(seed_tile, offsets):
    return sign_of(mix_tile(seed_tile, offsets))


def hash_kernel(seeds_ref, offsets_ref, grads_ref, out_ref, wide_ref):
    e_all, p_local = grads_ref.shape
    wide_ref[...] = jnp.broadcast_to(seeds_ref[...], wide_ref.shape)

    @pl.loop(0, out_ref.shape[1] // TILE)
    def _(block):
        columns = pl.ds(pl.multiple_of(block * TILE, TILE), TILE)
        offsets = offsets_ref[:, columns]

        def add(part, total):
            rows = pl.ds(pl.multiple_of(part * TILE, TILE), TILE)
            seed_tile = wide_ref[rows, :]
            halves = [sign_tile(seed_tile, offsets[:, i : i + 128]) for i in range(0, TILE, 128)]
            return total + jnp.dot(
                grads_ref[:, rows], jnp.concatenate(halves, axis=1), preferred_element_type=jnp.float32
            )

        out_ref[:, columns] = lax.fori_loop(
            0, p_local // TILE, add, jnp.zeros((e_all, TILE), jnp.float32)
        )


def features_of(example, n_c, n_e):
    width = K // (n_c * n_e)
    owner = jnp.arange(n_c, dtype=jnp.int32)[:, None] * (width * n_e)
    return (owner + example * width + jnp.arange(width, dtype=jnp.int32)[None, :]).reshape(1, -1)


def separate(grads, seeds, adam_table, ckpt_index):
    e_local, p_local = grads.shape
    n_c, n_e = lax.axis_size(("param", "sub")), lax.axis_size("example")
    p_whole = p_local * n_c
    width = K // (n_c * n_e)
    example = lax.axis_index("example")
    everyone = lax.all_gather(grads, "example", axis=0, tiled=True)
    index = lax.all_gather(ckpt_index, "example", axis=0, tiled=True)
    e_all = e_local * n_e
    partial = pl.pallas_call(
        hash_kernel,
        out_shape=jax.ShapeDtypeStruct((e_all, n_c * width), jnp.float32),
        in_specs=[pl.BlockSpec(memory_space=pltpu.VMEM)] * 3,
        out_specs=pl.BlockSpec(memory_space=pltpu.VMEM),
        scratch_shapes=[pltpu.VMEM((p_local, 128), jnp.int32)],
        compiler_params=pltpu.CompilerParams(vmem_limit_bytes=40 << 20),
    )(seeds[:, None], features_of(example, n_c, n_e) * jnp.int32(STEP), everyone)
    summed = lax.psum_scatter(partial, ("param", "sub"), scatter_dimension=1, tiled=True)
    projected = summed * (1.0 / math.sqrt(p_whole))
    table = lax.dynamic_slice_in_dim(adam_table, example * width, width, 1)
    onehot = (index[:, None] == jnp.arange(CKPT, dtype=jnp.int32)[None, :]).astype(jnp.float32)
    scale = jnp.dot(onehot, table, precision=lax.Precision.HIGHEST)
    plain = projected.astype(jnp.bfloat16)
    scaled = (projected * scale).astype(jnp.bfloat16)
    pairs = lax.dot_general(scaled, plain, (((1,), (1,)), ((), ())), preferred_element_type=jnp.float32)
    pairs = lax.psum_scatter(pairs, "example", scatter_dimension=0, tiled=True)
    pairs = lax.psum_scatter(pairs, ("param", "sub"), scatter_dimension=1, tiled=True)
    influence = pairs * (1.0 / math.sqrt(K))
    cols = pairs.shape[1]
    row_ids = example * e_local + jnp.arange(e_local, dtype=jnp.int32)
    col_ids = lax.axis_index(("param", "sub")) * cols + jnp.arange(cols, dtype=jnp.int32)
    return jnp.where(row_ids[:, None] == col_ids[None, :], jnp.zeros_like(influence), influence)


def flipped(index, mask, size):
    bits = [1 << i for i in range((size - 1).bit_length())]
    return sum((((index // b) % 2 + (mask // b) % 2) % 2) * b for b in bits) if bits else index


def fused_kernel(
    sizes, seeds_hbm, table_hbm, index_hbm, grads_hbm, out_ref,
    seeds_ref, table_ref, mixed_ref, load_sems, wide_ref, all_ref, who_ref, part_ref, fresh_ref, held_ref, near_ref, far_ref, thin_ref, thin_far_ref, scale_ref, pair_ref, block_ref,
    grad_send, grad_recv, who_send, who_recv, near_send, near_recv, far_send, far_recv, pair_send, pair_recv,
):
    n_p, n_e, n_s, p_whole = sizes
    n_c = n_p * n_s
    e_local, p_local = grads_hbm.shape
    e_all = n_e * e_local
    width = part_ref.shape[2]
    cols = out_ref.shape[0]
    piece = p_local // PIECES
    param, example, sub = lax.axis_index("param"), lax.axis_index("example"), lax.axis_index("sub")
    me = param * n_s + sub

    def device(c_mask, e_mask):
        return {
            "param": flipped(param, c_mask // n_s, n_p),
            "example": flipped(example, e_mask, n_e),
            "sub": flipped(sub, c_mask % n_s, n_s),
        }

    mine = pl.ds(pl.multiple_of(example * e_local, e_local), e_local)
    loads = [
        pltpu.make_async_copy(source, target, load_sems.at[i])
        for i, (source, target) in enumerate((
            (seeds_hbm, seeds_ref),
            (grads_hbm, all_ref.at[mine]),
            (index_hbm, who_ref.at[example]),
            (table_hbm, table_ref),
        ))
    ]
    for load in loads:
        load.start()
    barrier = pltpu.get_barrier_semaphore()
    for mask in range(1, n_c * n_e):
        pl.semaphore_signal(barrier, inc=1, device_id=device(mask % n_c, mask // n_c), device_id_type=MESH)

    def offsets_of(c_mask, block):
        first = (flipped(me, c_mask, n_c) * n_e + example) * width + block * TILE
        return (first + lax.broadcasted_iota(jnp.int32, (1, TILE), 1)) * jnp.int32(STEP)

    def signs_of(seed_tile, offsets):
        return jnp.concatenate(
            [sign_tile(seed_tile, offsets[:, i : i + 128]) for i in range(0, TILE, 128)], axis=1
        )

    def keep(slot, rows, seed_tile, offsets):
        for i in range(0, TILE, 128):
            mixed_ref[slot, rows, i : i + 128] = mix_tile(seed_tile, offsets[:, i : i + 128])

    last = n_c - 1
    loads[0].wait()
    turned = seeds_ref[...].T
    offsets = offsets_of(last, 1)
    for row in range(p_local // 128):
        rows = slice(row * 128, (row + 1) * 128)
        seed_tile = jnp.broadcast_to(turned[:, row : row + 1], (128, 128))
        wide_ref[rows, :] = seed_tile
        keep(0, rows, seed_tile, offsets)
    def keep_signs(begin, end):
        @pl.loop(begin, end)
        def _(slot):
            keep(slot, slice(0, p_local), wide_ref[...], offsets_of(last - slot, lax.rem(slot + 1, 2)))

    keep_signs(1, GREETED)
    pl.semaphore_wait(barrier, n_c * n_e - 1)
    grad_copies, who_copies = [], []
    for mask in range(1, n_e):
        copy = pltpu.make_async_remote_copy(
            src_ref=index_hbm, dst_ref=who_ref.at[example], send_sem=who_send.at[mask - 1],
            recv_sem=who_recv.at[mask - 1], device_id=device(0, mask), device_id_type=MESH,
        )
        who_copies.append(copy)
        for i in range(PIECES):
            span = pl.ds(i * piece, piece)
            copy = pltpu.make_async_remote_copy(
                src_ref=grads_hbm.at[:, span], dst_ref=all_ref.at[mine, span],
                send_sem=grad_send.at[mask - 1, i], recv_sem=grad_recv.at[mask - 1, i],
                device_id=device(0, mask), device_id_type=MESH,
            )
            grad_copies.append((i, copy))
    for copy in who_copies:
        copy.start()


    def grads_leave(half):
        for number, copy in grad_copies:
            if number // (PIECES // 2) == half:
                copy.start()

    grads_leave(0)
    keep_signs(GREETED, 2)
    grads_leave(1)
    keep_signs(2, KEPT)
    for load in loads[1:]:
        load.wait()

    def near_copy(z_mask):
        return pltpu.make_async_remote_copy(
            src_ref=part_ref.at[z_mask * 2 + 1], dst_ref=near_ref.at[z_mask], send_sem=near_send.at[z_mask],
            recv_sem=near_recv.at[z_mask], device_id=device(1, 0), device_id_type=MESH,
        )

    def far_copy(z_mask):
        source, target = part_ref.at[z_mask * 2], far_ref.at[z_mask - 1]
        if z_mask >= THIN:
            source, target = thin_ref.at[z_mask - THIN], thin_far_ref.at[z_mask - THIN]
        return pltpu.make_async_remote_copy(
            src_ref=source, dst_ref=target, send_sem=far_send.at[z_mask - 1],
            recv_sem=far_recv.at[z_mask - 1], device_id=device(z_mask * 2, 0), device_id_type=MESH,
        )

    def join(z_mask):
        near_copy(z_mask).wait_recv()
        total = part_ref[z_mask * 2] + near_ref[z_mask]
        if z_mask >= THIN:
            thin_ref[z_mask - THIN] = total.astype(jnp.bfloat16)
        else:
            part_ref[z_mask * 2] = total
        far_copy(z_mask).start()

    def fresh(c_mask, block, begin):
        rows = pl.ds(begin, SEGMENT)
        return jnp.dot(
            all_ref[:, rows], signs_of(wide_ref[rows, :], offsets_of(c_mask, block)), preferred_element_type=jnp.float32
        )

    def kept(slot, begin):
        rows = pl.ds(begin, SEGMENT)
        return jnp.dot(all_ref[:, rows], sign_of(mixed_ref[slot, rows, :]), preferred_element_type=jnp.float32)

    def segments(slot, parity, begin, end):
        for row in range(begin, end, SEGMENT):
            for block, ref, term in (
                (parity, fresh_ref, lambda: fresh(last - slot, parity, row)),
                (1 - parity, held_ref, lambda: kept(slot, row)),
            ):
                total = term()
                if row > 0:
                    total = total + ref[parity]
                if row + SEGMENT < p_local:
                    ref[parity] = total
                else:
                    part_ref[last - slot, :, block * TILE : (block + 1) * TILE] = total

    def grads_arrive(half):
        for number, copy in grad_copies:
            if number // (PIECES // 2) == half:
                copy.wait_recv()

    middle = p_local // 2
    for half in range(2):
        grads_arrive(half)
        for parity in range(2):
            segments(parity, parity, half * middle, (half + 1) * middle)
    near_copy(n_p - 1).start()
    for copy in who_copies:
        copy.wait_recv()
    own = pl.ds(pl.multiple_of(example * width, 128), width)
    who = jnp.concatenate(
        [jnp.broadcast_to(who_ref[i], (8, e_local)).T[:, 0:1] for i in range(n_e)], axis=0
    )
    scale = jnp.zeros((e_all, width), jnp.float32)
    for row in range(CKPT):
        scale = jnp.where(who == row, table_ref[row : row + 1, own], scale)
    scale_ref[...] = scale

    @pl.loop(1, n_p - 1)
    def _(group):
        segments(group * 2, 0, 0, middle)

        @pl.when(group == 1)
        def _():
            join(n_p - 1)

        segments(group * 2, 0, middle, p_local)
        near_copy(n_p - 1 - group).start()
        segments(group * 2 + 1, 1, 0, p_local)

        for z_mask in range(1, n_p - 1):
            @pl.when(group == n_p - 1 - z_mask)
            def _():
                join(z_mask)

    segments(last - 1, 0, 0, p_local)
    near_copy(0).start()

    @pl.loop(0, 2)
    def _(block):
        span = pl.ds(pl.multiple_of(block * TILE, TILE), TILE)
        part_ref[0, :, span] = jnp.dot(
            all_ref[...], signs_of(wide_ref[...], offsets_of(0, block)), preferred_element_type=jnp.float32
        )

    summed = part_ref[0]
    for z_mask in range(n_p - 1, 0, -1):
        far_copy(z_mask).wait_recv()
        landed = far_ref[z_mask - 1] if z_mask < THIN else thin_far_ref[z_mask - THIN].astype(jnp.float32)
        summed = summed + landed
    near_copy(0).wait_recv()
    summed = summed + near_ref[0]
    projected = summed * (1.0 / math.sqrt(p_whole))
    plain = projected.astype(jnp.bfloat16)
    scaled = (projected * scale_ref[...]).astype(jnp.bfloat16)
    lanes = pair_ref.shape[1]
    if lanes > e_all:
        scaled = jnp.concatenate([scaled, jnp.zeros((lanes - e_all, width), jnp.bfloat16)], axis=0)
    pair_ref[...] = lax.dot_general(
        plain, scaled, (((1,), (1,)), ((), ())), preferred_element_type=jnp.float32
    )

    copies = []
    for mask in range(n_c * n_e - 1, 0, -1):
        c_mask, e_mask = mask % n_c, mask // n_c
        rows = pl.ds(pl.multiple_of(flipped(me, c_mask, n_c) * cols, cols), cols)
        copy = pltpu.make_async_remote_copy(
            src_ref=pair_ref.at[rows], dst_ref=block_ref.at[mask - 1], send_sem=pair_send.at[mask - 1],
            recv_sem=pair_recv.at[mask - 1], device_id=device(c_mask, e_mask), device_id_type=MESH,
        )
        copy.start()
        copies.append((mask, copy))
    pairs = pair_ref[pl.ds(pl.multiple_of(me * cols, cols), cols), :]
    for mask, copy in copies[::-1]:
        copy.wait_recv()
        pairs = pairs + block_ref[mask - 1]
    block = pairs[:, :e_local]
    for i in range(1, n_e):
        block = jnp.where(example == i, pairs[:, i * e_local : (i + 1) * e_local], block)
    block = block * (1.0 / math.sqrt(K))
    col_ids = me * cols + lax.broadcasted_iota(jnp.int32, block.shape, 0)
    row_ids = example * e_local + lax.broadcasted_iota(jnp.int32, block.shape, 1)
    out_ref[...] = jnp.where(row_ids == col_ids, jnp.zeros_like(block), block)
    for mask, copy in copies:
        copy.wait_send()
    for z_mask in range(n_p):
        near_copy(z_mask).wait_send()
    for z_mask in range(1, n_p):
        far_copy(z_mask).wait_send()
    for number, copy in grad_copies:
        copy.wait_send()
    for copy in who_copies:
        copy.wait_send()


def fused(grads, seeds, adam_table, ckpt_index):
    e_local, p_local = grads.shape
    n_p, n_e, n_s = (lax.axis_size(name) for name in ("param", "example", "sub"))
    n_c = n_p * n_s
    e_all = e_local * n_e
    width = K // (n_c * n_e)
    cols = e_all // n_c
    lanes = -(-e_all // 128) * 128
    dma = pltpu.SemaphoreType.DMA
    return pl.pallas_call(
        functools.partial(fused_kernel, (n_p, n_e, n_s, p_local * n_c)),
        out_shape=pltpu.VMEM((cols, e_local), jnp.float32),
        in_specs=[pl.BlockSpec(memory_space=pltpu.HBM)] * 4,
        out_specs=pl.BlockSpec(memory_space=pltpu.VMEM),
        scratch_shapes=[
            pltpu.VMEM((p_local // 128, 128), jnp.int32),
            pltpu.VMEM(adam_table.shape, jnp.float32),
            pltpu.VMEM((KEPT, p_local, TILE), jnp.int32),
            dma((4,)),
            pltpu.VMEM((p_local, 128), jnp.int32),
            pltpu.VMEM((e_all, p_local), jnp.bfloat16),
            pltpu.VMEM((n_e, 1, e_local), jnp.int32),
            pltpu.VMEM((n_c, e_all, width), jnp.float32),
            pltpu.VMEM((2, e_all, TILE), jnp.float32),
            pltpu.VMEM((2, e_all, TILE), jnp.float32),
            pltpu.VMEM((n_p, e_all, width), jnp.float32),
            pltpu.VMEM((n_p - 1, e_all, width), jnp.float32),
            pltpu.VMEM((n_p - THIN, e_all, width), jnp.bfloat16),
            pltpu.VMEM((n_p - THIN, e_all, width), jnp.bfloat16),
            pltpu.VMEM((e_all, width), jnp.float32),
            pltpu.VMEM((e_all, lanes), jnp.float32),
            pltpu.VMEM((n_c * n_e - 1, cols, lanes), jnp.float32),
            dma((n_e - 1, PIECES)),
            dma((n_e - 1, PIECES)),
            dma((n_e - 1,)),
            dma((n_e - 1,)),
            dma((n_p,)),
            dma((n_p,)),
            dma((n_p - 1,)),
            dma((n_p - 1,)),
            dma((n_c * n_e - 1,)),
            dma((n_c * n_e - 1,)),
        ],
        compiler_params=pltpu.CompilerParams(
            collective_id=0, has_side_effects=True, vmem_limit_bytes=58720256
        ),
    )(
        seeds.reshape(p_local // 128, 128),
        adam_table,
        ckpt_index.reshape(1, e_local),
        grads,
    ).T


def per_device(grads, seeds, adam_table, ckpt_index):
    e_local, p_local = grads.shape
    n_c, n_e = lax.axis_size(("param", "sub")), lax.axis_size("example")
    width, cols = K // (n_c * n_e), e_local * n_e // n_c
    n_p, n_s = lax.axis_size("param"), lax.axis_size("sub")
    if (n_p, n_e, n_s) == (4, 2, 2) and width == 2 * TILE and p_local == 2 * ROWS and cols % 8 == 0:
        return fused(grads, seeds, adam_table, ckpt_index)
    return separate(grads, seeds, adam_table, ckpt_index)


def solution(mesh):
    placed = (
        P(("groups", "example"), ("param", "sub")),
        P(("groups", "param", "sub")),
        P(None, ("groups", "param", "sub")),
        P(("groups", "example")),
    )
    return jax.shard_map(
        per_device,
        mesh=mesh,
        in_specs=placed,
        out_specs=P(("groups", "example"), ("param", "sub")),
        check_vma=False,
    )
```
